32 devices in a mesh: dp: 4 (over y, x), ctx: 8 (over z, core).
Axes of the slice: x: 2, y: 2, z: 4, core: 2. Of those that a mesh axis runs over, the one named last changes fastest.
Arguments:
- query_matrix: bfloat16 [4, 1024, 2048], P('dp', 'ctx'), may hold values from -16 to 16
- key_matrix: bfloat16 [4, 1024, 512], P('dp', 'ctx'), may hold values from -16 to 16
- value_matrix: bfloat16 [4, 1024, 512], P('dp', 'ctx'), may hold values from -6 to 6
- output_gradient: bfloat16 [4, 1024, 2048], P('dp', 'ctx'), may hold values from -6 to 6
- hidden_in: bfloat16 [4, 1024, 4096], P('dp', 'ctx'), may hold values from -6 to 6
- doc_lengths: int32 [4, 16], P('dp'), may hold values from 1 to 768, 1024 in all within a row
- querya: bfloat16 [16, 4096], replicated, may hold values from -0.09375 to 0.09375
- queryb: bfloat16 [16, 2048], replicated, may hold values from -1.5 to 1.5
- valuea: bfloat16 [16, 4096], replicated, may hold values from -0.09375 to 0.09375
- valueb: bfloat16 [16, 512], replicated, may hold values from -1.5 to 1.5
Outputs:
- query_grad: bfloat16 [4, 1024, 2048], P('dp', 'ctx')
- key_grad: bfloat16 [4, 1024, 512], P('dp', 'ctx')
- value_gradient: bfloat16 [4, 1024, 512], P('dp', 'ctx')
- querya_grad: float32 [16, 4096], replicated
- queryb_grad: float32 [16, 2048], replicated
- valuea_grad: float32 [16, 4096], replicated
- valueb_grad: float32 [16, 512], replicated
The draws below stay inside these ranges and needn't reach their ends.
Inputs may be any that keep to these rules, and one draw needn't show every extreme that they name: `doc_lengths`: row b lists, in order, the lengths of the 16 documents packed into sequence b; they sum to 1024.
All inputs are finite; a program needn't handle non-finite values.
Results may differ from the reference program's by a relative error of at most 0.022.
Values may be sent and summed in bfloat16 or wider, within the bound.
No kernel may reach another device: no remote copies, remote signals or barrier semaphores. Data moves between devices by JAX's collectives and lax.ppermute only.
A program may use at most 128 MiB of HBM per device.

```python
import math
import jax
import jax.numpy as jnp
import numpy as np
from jax import lax

D = 4096
QUERY_HEADS = 16
KEY_VALUE_HEADS = 4
HEAD_WIDTH = 128
ADAPTER_RANK = 16
DOCS = 16
TOKENS_PER_SHARD = 128
SEQUENCE_LENGTH = 1024
BATCH_SEQUENCES = 4
N_CTX = 8


def paired_fields(key):
    base_key = jax.random.fold_in(key, 31)
    random_query, random_keys = jax.random.split(base_key, 2)
    group_width = QUERY_HEADS // KEY_VALUE_HEADS
    query_list = jnp.clip(jax.random.normal(random_query, (BATCH_SEQUENCES, SEQUENCE_LENGTH, KEY_VALUE_HEADS, group_width, HEAD_WIDTH), jnp.float32), -4.0, 4.0)
    key_collection = jnp.clip(jax.random.normal(random_keys, (BATCH_SEQUENCES, SEQUENCE_LENGTH, KEY_VALUE_HEADS, HEAD_WIDTH), jnp.float32), -3.0, 3.0)
    return (query_list.reshape(BATCH_SEQUENCES, SEQUENCE_LENGTH, QUERY_HEADS * HEAD_WIDTH), key_collection.reshape(BATCH_SEQUENCES, SEQUENCE_LENGTH, KEY_VALUE_HEADS * HEAD_WIDTH))


def draw_query_matrix(key, part):
    return paired_fields(key)[0].astype(jnp.bfloat16)


def draw_key_matrix(key, part):
    return paired_fields(key)[1].astype(jnp.bfloat16)


def steps_of(own_key, dims, shards, low, high):
    def one(dim, shards_of):
        draws = jax.random.uniform(jax.random.fold_in(jax.random.fold_in(own_key, 6), dim), (shards_of,), jnp.float32, low / len(shards), high / len(shards))
        return jnp.repeat(jnp.exp(draws), dims[dim] // shards_of).reshape((-1,) + (1,) * (len(dims) - dim - 1))

    factor_of = one(*shards[0])
    for cut in shards[1:]:
        factor_of = factor_of * one(*cut)
    return factor_of


def profile(number_of, total, reach, slope):
    loads = [(1 << 20) // math.isqrt(grade ** slope) + 1 for grade in range(2, number_of + 1)]
    surplus, given = total - reach - (number_of - 1), [1] * (number_of - 1)
    while surplus > 0:
        free = [i for i in range(number_of - 1) if given[i] < reach]
        whole, left = sum([loads[i] for i in free]), surplus
        for i in free:
            extra = min(reach - given[i], max(1, left * loads[i] // whole), surplus)
            given[i] = given[i] + extra
            surplus = surplus - extra
    return np.array([reach] + given)


def uneven_parts(stream_key, amount, total, limit, skew):
    if amount == 2:
        one = jax.random.randint(stream_key, (), max(1, total - limit), min(limit, total - 1) + 1)
        return jnp.stack([one, total - one])
    sizes = jnp.asarray(profile(amount, total, limit, skew), jnp.int32)
    pairs = (amount - 1) // 2
    source_of, taker = sizes[1:1 + 2 * pairs:2], sizes[2:2 + 2 * pairs:2]
    slack = jnp.minimum(source_of - 1, limit - taker)
    passed = jax.random.randint(jax.random.fold_in(stream_key, 1), (pairs,), 0, 1 << 20) % (slack + 1)
    sizes = sizes.at[1:1 + 2 * pairs:2].set(source_of - passed).at[2:2 + 2 * pairs:2].set(taker + passed)
    return sizes[jax.random.permutation(jax.random.fold_in(stream_key, 2), amount)]


def noise(rng, shape, deviation, most, cuts=(), held_as=jnp.bfloat16):
    values = deviation * jax.random.normal(rng, shape, jnp.float32)
    if cuts:
        values = values * steps_of(rng, shape, cuts, -0.22, 0.18)
    return jnp.clip(values, -most, most).astype(held_as)


def setup_inputs(seed: int = 0) -> dict:
    arg_keys = jax.random.split(jax.random.key(seed), 11)
    query_matrix = draw_query_matrix(jax.random.fold_in(arg_keys[10], 71), 0)
    key_matrix = draw_key_matrix(jax.random.fold_in(arg_keys[10], 71), 0)
    value_matrix = noise(arg_keys[2], (BATCH_SEQUENCES, SEQUENCE_LENGTH, KEY_VALUE_HEADS * HEAD_WIDTH), 1.0, 6.0, ((0, 4), (1, 8)))
    output_gradient = noise(arg_keys[3], (BATCH_SEQUENCES, SEQUENCE_LENGTH, QUERY_HEADS * HEAD_WIDTH), 1.0, 6.0, ((0, 4), (1, 8)))
    hidden_in = noise(arg_keys[4], (BATCH_SEQUENCES, SEQUENCE_LENGTH, D), 1.0, 6.0, ((0, 4), (1, 8)))
    doc_lengths = jax.vmap(lambda own: uneven_parts(own, DOCS, SEQUENCE_LENGTH, 3 * SEQUENCE_LENGTH // 4, 2))(jax.random.split(arg_keys[5], BATCH_SEQUENCES)).reshape((BATCH_SEQUENCES, DOCS)).astype(jnp.int32)
    querya = noise(arg_keys[6], (ADAPTER_RANK, D), D ** -0.5, 0.09375)
    queryb = noise(arg_keys[7], (ADAPTER_RANK, QUERY_HEADS * HEAD_WIDTH), ADAPTER_RANK ** -0.5, 1.5)
    valuea = noise(arg_keys[8], (ADAPTER_RANK, D), D ** -0.5, 0.09375)
    valueb = noise(arg_keys[9], (ADAPTER_RANK, KEY_VALUE_HEADS * HEAD_WIDTH), ADAPTER_RANK ** -0.5, 1.5)
    return dict(query_matrix=query_matrix, key_matrix=key_matrix, value_matrix=value_matrix, output_gradient=output_gradient, hidden_in=hidden_in, doc_lengths=doc_lengths, querya=querya, queryb=queryb, valuea=valuea, valueb=valueb)


NEG_FILL = -1.0e30
ADAPTER_SCALE = 2.0


def doc_begin(lengths, positions):
    doc_ends = jnp.cumsum(lengths).astype(jnp.int32)
    begins = (doc_ends - lengths).astype(jnp.int32)
    inside = begins[None, :] <= positions[:, None]
    return jnp.max(jnp.where(inside, begins[None, :], 0), axis=1).astype(jnp.int32)


def rounded_length(values):
    return lax.optimization_barrier(values.astype(jnp.bfloat16)).astype(jnp.float32)


def contract_last(left, right):
    return lax.dot_general(left, right, (((1,), (1,)), ((), ())), preferred_element_type=jnp.float32)


def contract_first(left, right):
    return lax.dot_general(left, right, (((0,), (0,)), ((), ())), preferred_element_type=jnp.float32)


def sequence_grads(packed):
    query_matrix, key_matrix, value_matrix, output_gradient, lengths = packed
    sequence_total = TOKENS_PER_SHARD * N_CTX
    group_width = QUERY_HEADS // KEY_VALUE_HEADS
    rows_per_half = TOKENS_PER_SHARD // 2
    head_scale = HEAD_WIDTH ** -0.5
    positions = lax.iota(jnp.int32, sequence_total)
    begins = doc_begin(lengths, positions)
    key_quad = key_matrix.reshape(sequence_total, KEY_VALUE_HEADS, HEAD_WIDTH).astype(jnp.float32)
    value_quad = value_matrix.reshape(sequence_total, KEY_VALUE_HEADS, HEAD_WIDTH).astype(jnp.float32)
    query_block_list = query_matrix.reshape(N_CTX, TOKENS_PER_SHARD, KEY_VALUE_HEADS, group_width, HEAD_WIDTH)
    gradient_block_list = output_gradient.reshape(N_CTX, TOKENS_PER_SHARD, KEY_VALUE_HEADS, group_width, HEAD_WIDTH)
    pos_blocks = positions.reshape(N_CTX, TOKENS_PER_SHARD)
    begin_blocks = begins.reshape(N_CTX, TOKENS_PER_SHARD)

    def one_block(carry_in, inputs):
        key_total_sum, value_total_sum = carry_in
        query_block, grad_block, pos_block, begin_block = inputs
        query_wide = query_block.astype(jnp.float32)
        gradient_wide = grad_block.astype(jnp.float32)
        visible = ((positions[None, :] <= pos_block[:, None]) & (positions[None, :] >= begin_block[:, None]))[:, None, None, :]
        scores = jnp.einsum("thgd,chd->thgc", query_wide, key_quad) * head_scale
        row_max = jnp.max(jnp.where(visible, scores, NEG_FILL), axis=-1)
        unnorm = jnp.where(visible, jnp.exp(scores - row_max[..., None]), 0.0)
        row_total = jnp.sum(unnorm, axis=-1)
        attended = jnp.einsum("thgc,chd->thgd", rounded_length(unnorm), value_quad) / row_total[..., None]
        log_total = row_max + jnp.log(row_total)
        delta_rows = jnp.sum(gradient_wide * attended, axis=-1)
        probabilities = jnp.where(visible, jnp.exp(scores - log_total[..., None]), 0.0)
        grad_probs = jnp.einsum("thgd,chd->thgc", gradient_wide, value_quad)
        score_gradient = rounded_length(probabilities * (grad_probs - delta_rows[..., None]) * head_scale)
        query_grad = jnp.einsum("thgc,chd->thgd", score_gradient, key_quad).astype(jnp.bfloat16)
        score_split_halves = score_gradient.reshape(2, rows_per_half, KEY_VALUE_HEADS, group_width, sequence_total)
        probability_halves = rounded_length(probabilities).reshape(2, rows_per_half, KEY_VALUE_HEADS, group_width, sequence_total)
        query_split_halves = query_wide.reshape(2, rows_per_half, KEY_VALUE_HEADS, group_width, HEAD_WIDTH)
        gradient_halves = gradient_wide.reshape(2, rows_per_half, KEY_VALUE_HEADS, group_width, HEAD_WIDTH)
        key_part = jnp.sum(rounded_length(jnp.einsum("pthgc,pthgd->pchd", score_split_halves, query_split_halves)), axis=0)
        value_part = jnp.sum(rounded_length(jnp.einsum("pthgc,pthgd->pchd", probability_halves, gradient_halves)), axis=0)
        return (key_total_sum + key_part, value_total_sum + value_part), query_grad

    zero_sum_start = jnp.zeros((sequence_total, KEY_VALUE_HEADS, HEAD_WIDTH), jnp.float32)
    (key_total_sum, value_total_sum), query_grads = lax.scan(one_block, (zero_sum_start, zero_sum_start), (query_block_list, gradient_block_list, pos_blocks, begin_blocks))
    return (query_grads.reshape(sequence_total, QUERY_HEADS * HEAD_WIDTH),
            key_total_sum.reshape(sequence_total, KEY_VALUE_HEADS * HEAD_WIDTH).astype(jnp.bfloat16),
            value_total_sum.reshape(sequence_total, KEY_VALUE_HEADS * HEAD_WIDTH).astype(jnp.bfloat16))


def reference(query_matrix, key_matrix, value_matrix, output_gradient, hidden_in, doc_lengths, querya, queryb, valuea, valueb):
    query_grad, key_grad, value_gradient = lax.map(sequence_grads, (query_matrix, key_matrix, value_matrix, output_gradient, doc_lengths))
    tokens_in = hidden_in.reshape(-1, D)
    flat_query = query_grad.reshape(-1, QUERY_HEADS * HEAD_WIDTH)
    flattened_value = value_gradient.reshape(-1, KEY_VALUE_HEADS * HEAD_WIDTH)
    query_proj = contract_last(tokens_in, querya).astype(jnp.bfloat16)
    value_proj = contract_last(tokens_in, valuea).astype(jnp.bfloat16)
    query_low = contract_last(flat_query, queryb).astype(jnp.bfloat16)
    value_low = contract_last(flattened_value, valueb).astype(jnp.bfloat16)
    querya_grad = ADAPTER_SCALE * contract_first(query_low, tokens_in)
    queryb_grad = ADAPTER_SCALE * contract_first(query_proj, flat_query)
    valuea_grad = ADAPTER_SCALE * contract_first(value_low, tokens_in)
    valueb_grad = ADAPTER_SCALE * contract_first(value_proj, flattened_value)
    return (query_grad, key_grad, value_gradient, querya_grad, queryb_grad, valuea_grad, valueb_grad)
```

```python
import functools

import jax
import jax.numpy as jnp
from jax import lax
from jax.experimental import pallas as pl
from jax.experimental.pallas import tpu as pltpu
from jax.sharding import PartitionSpec as P

QUERY_HEADS = 16
KEY_VALUE_HEADS = 4
HEAD_WIDTH = 128
NEG_FILL = -1e30
ADAPTER_SCALE = 2.0


F32 = jnp.float32
BF16 = jnp.bfloat16
VM = pl.BlockSpec(memory_space=pltpu.VMEM)
SM = pl.BlockSpec(memory_space=pltpu.SMEM)

CORE_HEADS = KEY_VALUE_HEADS // 2
GROUP = QUERY_HEADS // KEY_VALUE_HEADS
Q_HALF = QUERY_HEADS * HEAD_WIDTH // 2
KV_HALF = CORE_HEADS * HEAD_WIDTH


def dot_nn(a, b):
    return lax.dot_general(a, b, (((1,), (0,)), ((), ())), preferred_element_type=F32)


def dot_nt(a, b):
    return lax.dot_general(a, b, (((1,), (1,)), ((), ())), preferred_element_type=F32)


def dot_tn(a, b):
    return lax.dot_general(a, b, (((0,), (0,)), ((), ())), preferred_element_type=F32)


def half_of(ref, core, width):
    return ref[:, pl.ds(pl.multiple_of(core * width, 128), width)]


def call(body, outs, args, scratch=(), flops=0, smem=()):
    size = sum(a.size * a.dtype.itemsize for a in args)
    size += sum(o.size * o.dtype.itemsize for o in outs)
    return pl.pallas_call(
        body,
        out_shape=outs,
        in_specs=[SM if i in smem else VM for i in range(len(args))],
        out_specs=[VM] * len(outs),
        scratch_shapes=list(scratch),
        compiler_params=pltpu.CompilerParams(vmem_limit_bytes=60 << 20),
        cost_estimate=pl.CostEstimate(flops=flops, bytes_accessed=size, transcendentals=0),
    )(*args)


def split_kv(k_ref, v_ref, own_ref, send_ref):
    core = lax.axis_index("ctx") % 2
    for i, ref in enumerate((k_ref, v_ref)):
        columns = slice(i * KV_HALF, (i + 1) * KV_HALF)
        own_ref[:, columns] = half_of(ref, core, KV_HALF)
        send_ref[:, columns] = half_of(ref, 1 - core, KV_HALF)


def split_rest(q_ref, g_ref, hidden_ref, qa_ref, va_ref, send_ref, proj_ref):
    core = lax.axis_index("ctx") % 2
    width = hidden_ref.shape[1] // 2
    send_ref[:, :Q_HALF] = half_of(q_ref, 1 - core, Q_HALF)
    send_ref[:, Q_HALF : 2 * Q_HALF] = half_of(g_ref, 1 - core, Q_HALF)
    send_ref[:, 2 * Q_HALF :] = half_of(hidden_ref, 1 - core, width)
    rank = qa_ref.shape[0]
    proj_ref[:rank] = dot_nt(qa_ref[...], hidden_ref[...]).astype(BF16)
    proj_ref[rank:] = dot_nt(va_ref[...], hidden_ref[...]).astype(BF16)


def attention(n_chips, rank, *refs):
    lens_ref, q_ref, g_ref, pack_ref, own_proj_ref, far_proj_ref, qb_ref, vb_ref = refs[:8]
    kv_in = refs[8 : 8 + n_chips]
    vp_in = refs[8 + n_chips : 7 + 2 * n_chips]
    refs = refs[7 + 2 * n_chips :]
    dq_own_ref, dq_send_ref, low_ref, qbg_ref, vbg_ref = refs[:5]
    dkv_out = refs[5 : 5 + n_chips]
    vl_out = refs[5 + n_chips : 5 + 2 * n_chips]
    kv, vp, dkv, vl, s_ref, dp_ref, p_ref, ds_ref, qs, gs, dqt = refs[5 + 2 * n_chips :]
    rows = q_ref.shape[0]
    chip_rows = 2 * rows
    lanes = GROUP * chip_rows
    head_scale = HEAD_WIDTH ** (-0.5)
    index = lax.axis_index("ctx")
    core, chip = index % 2, index // 2

    for k in range(n_chips):
        kv[k] = kv_in[k][...]
    vp[0, :, :rows] = own_proj_ref[rank:]
    vp[0, :, rows:] = far_proj_ref[rank:]
    for k in range(1, n_chips):
        vp[k] = vp_in[k - 1][...]
    for i in range(CORE_HEADS * GROUP):
        g, j = i // GROUP, i % GROUP
        at = pl.multiple_of(core * Q_HALF + i * HEAD_WIDTH, 128)
        top = slice(j * chip_rows, j * chip_rows + rows)
        low = slice(j * chip_rows + rows, (j + 1) * chip_rows)
        qs[g, top] = q_ref[:, pl.ds(at, HEAD_WIDTH)]
        qs[g, low] = pack_ref[:, i * HEAD_WIDTH : (i + 1) * HEAD_WIDTH]
        gs[g, top] = g_ref[:, pl.ds(at, HEAD_WIDTH)]
        gs[g, low] = pack_ref[:, Q_HALF + i * HEAD_WIDTH : Q_HALF + (i + 1) * HEAD_WIDTH]
    dkv[...] = jnp.zeros_like(dkv)
    vl[...] = jnp.zeros_like(vl)

    def local(t):
        return jnp.where(t < rows, core * rows + t, (1 - core) * rows + t - rows)

    row_pos = chip * chip_rows + local(lax.broadcasted_iota(jnp.int32, (1, chip_rows), 1))
    row_begin = jnp.zeros_like(row_pos)
    first_pos = chip * chip_rows
    first_begin = jnp.int32(0)
    begin = jnp.int32(0)
    for i in range(lens_ref.shape[1]):
        row_begin = jnp.where(row_pos >= begin, jnp.maximum(row_begin, begin), row_begin)
        first_begin = jnp.where(first_pos >= begin, jnp.maximum(first_begin, begin), first_begin)
        begin = begin + lens_ref[0, i]
    key_local = local(lax.broadcasted_iota(jnp.int32, (chip_rows, 1), 0))
    reach = (first_pos - first_begin + chip_rows - 1) // chip_rows + 1
    seen = jnp.minimum(reach, chip + 1)

    def one_group(g, _):
        at_k = pl.multiple_of(g * HEAD_WIDTH, 128)
        at_v = pl.multiple_of(KV_HALF + g * HEAD_WIDTH, 128)

        def scores(k, top):
            keys = kv[k, :, pl.ds(at_k, HEAD_WIDTH)]
            key_pos = (chip - k) * chip_rows + key_local
            visible = (key_pos <= row_pos) & (key_pos >= row_begin)
            new = []
            for j in range(GROUP):
                part = slice(j * chip_rows, (j + 1) * chip_rows)
                s = dot_nt(keys, qs[g, part]) * head_scale
                s = jnp.where(visible, s, NEG_FILL)
                s_ref[k, :, part] = s
                new.append(jnp.maximum(top[j], jnp.max(s, axis=0, keepdims=True)))
            return tuple(new)

        top = lax.fori_loop(
            0, seen, scores, (jnp.full((1, chip_rows), NEG_FILL, F32),) * GROUP
        )

        def totals(k, carry):
            values = kv[k, :, pl.ds(at_v, HEAD_WIDTH)]
            new = []
            for j in range(GROUP):
                part = slice(j * chip_rows, (j + 1) * chip_rows)
                e = jnp.exp(s_ref[k, :, part] - top[j])
                dp = dot_nt(values, gs[g, part])
                s_ref[k, :, part] = e
                dp_ref[k, :, part] = dp
                total, delta = carry[j]
                new.append(
                    (
                        total + jnp.sum(e, axis=0, keepdims=True),
                        delta + jnp.sum(e * dp, axis=0, keepdims=True),
                    )
                )
            return tuple(new)

        zero = jnp.zeros((1, chip_rows), F32)
        sums = lax.fori_loop(0, seen, totals, ((zero, zero),) * GROUP)
        inverse = [1.0 / total for total, _ in sums]
        delta = [d * i for (_, d), i in zip(sums, inverse)]
        dqt[...] = jnp.zeros_like(dqt)

        def gradients(k, _):
            keys = kv[k, :, pl.ds(at_k, HEAD_WIDTH)]
            for j in range(GROUP):
                part = slice(j * chip_rows, (j + 1) * chip_rows)
                p = s_ref[k, :, part] * inverse[j]
                p_ref[:, part] = p.astype(BF16)
                ds = p * (dp_ref[k, :, part] - delta[j]) * head_scale
                ds_ref[:, part] = ds.astype(BF16)
            ds = ds_ref[...]
            dv = dot_nn(p_ref[...], gs[g]).astype(BF16)
            dkv[k, :, pl.ds(at_k, HEAD_WIDTH)] = dot_nn(ds, qs[g]).astype(BF16)
            dkv[k, :, pl.ds(at_v, HEAD_WIDTH)] = dv
            dqt[...] += dot_tn(keys, ds)
            at_b = pl.multiple_of(core * KV_HALF + g * HEAD_WIDTH, 128)
            vl[k] += dot_nt(vb_ref[:, pl.ds(at_b, HEAD_WIDTH)], dv)
            return 0

        lax.fori_loop(0, seen, gradients, 0)
        at_b = pl.multiple_of(core * Q_HALF + g * GROUP * HEAD_WIDTH, 128)
        qp_own, qp_far = own_proj_ref[:rank], far_proj_ref[:rank]
        for j in range(GROUP):
            part = dqt[:, j * chip_rows : (j + 1) * chip_rows].astype(BF16)
            up = qb_ref[:, pl.ds(pl.multiple_of(at_b + j * HEAD_WIDTH, 128), HEAD_WIDTH)]
            low = dot_nn(up, part)
            low_ref[...] = jnp.where((g == 0) & (j == 0), low, low_ref[...] + low)
            dq = jnp.transpose(dqt[:, j * chip_rows : (j + 1) * chip_rows]).astype(BF16)
            at = pl.ds(pl.multiple_of((g * GROUP + j) * HEAD_WIDTH, 128), HEAD_WIDTH)
            dq_own_ref[:, at] = dq[:rows]
            dq_send_ref[:, at] = dq[rows:]
            qbg_ref[:, at] = dot_nn(qp_own, dq[:rows]) + dot_nn(qp_far, dq[rows:])
        return 0

    low_ref[...] = jnp.zeros_like(low_ref)
    lax.fori_loop(0, CORE_HEADS, one_group, 0)
    total = jnp.zeros(vbg_ref.shape, F32)
    for k in range(n_chips):
        total = total + dot_nn(vp[k], dkv[k, :, KV_HALF:])
        dkv_out[k][...] = dkv[k]
        vl_out[k][...] = vl[k]
    vbg_ref[...] = total


def adapters(n_dp, rank, own_ref, far_ref, hidden_ref, pack_ref, qbg_ref, vbg_ref, *refs):
    outs, buffer = refs[:n_dp], refs[n_dp]
    core = lax.axis_index("ctx") % 2
    place = lax.axis_index("dp")
    rows = hidden_ref.shape[0]
    width = hidden_ref.shape[1] // 2
    near = (own_ref[:, :rows] + far_ref[:, rows:]).astype(BF16)
    away = (own_ref[:, rows:] + far_ref[:, :rows]).astype(BF16)
    both = dot_nn(near, half_of(hidden_ref, core, width)) + dot_nn(away, pack_ref[:, 2 * Q_HALF :])
    both = (ADAPTER_SCALE * both).astype(BF16)
    buffer[...] = jnp.zeros_like(buffer)
    buffer[:, :width] = both[:rank]
    buffer[:, width : 2 * width] = both[rank:]
    at = 2 * width
    buffer[:, at : at + Q_HALF] = (ADAPTER_SCALE * qbg_ref[...]).astype(BF16)
    at += Q_HALF
    buffer[:, at : at + KV_HALF] = (ADAPTER_SCALE * vbg_ref[...]).astype(BF16)
    piece = outs[0].shape[1]
    for k in range(n_dp):
        outs[k][...] = half_of(buffer, place ^ k, piece)


def finish_adapters(n_dp, rank, width, *refs):
    own, far = refs[:n_dp], refs[n_dp : 2 * n_dp]
    qa_ref, qb_ref, va_ref, vb_ref = refs[2 * n_dp : 2 * n_dp + 4]
    buffer = refs[2 * n_dp + 4]
    core = lax.axis_index("ctx") % 2
    place = lax.axis_index("dp")
    piece = own[0].shape[1]
    for side, pieces in ((0, own), (1, far)):
        half = core if side == 0 else 1 - core
        for k in range(n_dp):
            buffer[:, pl.ds(pl.multiple_of((place ^ k) * piece, 128), piece)] = pieces[k][...].astype(F32)
        at = 0
        for ref, wide in ((qa_ref, width), (va_ref, width), (qb_ref, Q_HALF), (vb_ref, KV_HALF)):
            ref[:, pl.ds(pl.multiple_of(half * wide, 128), wide)] = buffer[:, at : at + wide]
            at += wide


def join_rows(own_ref, far_ref, out_ref):
    core = lax.axis_index("ctx") % 2
    width = own_ref.shape[1]
    out_ref[:, pl.ds(pl.multiple_of(core * width, 128), width)] = own_ref[...]
    out_ref[:, pl.ds(pl.multiple_of((1 - core) * width, 128), width)] = far_ref[...]


def join_kv(own_ref, far_ref, dk_ref, dv_ref):
    core = lax.axis_index("ctx") % 2
    rows = far_ref.shape[0]
    for i, ref in enumerate((dk_ref, dv_ref)):
        columns = slice(i * KV_HALF, (i + 1) * KV_HALF)
        ref[:, pl.ds(pl.multiple_of(core * KV_HALF, 128), KV_HALF)] = own_ref[:rows, columns]
        ref[:, pl.ds(pl.multiple_of((1 - core) * KV_HALF, 128), KV_HALF)] = far_ref[:, columns]


def tree_sum(parts):
    while len(parts) > 1:
        parts = [a + b for a, b in zip(parts[::2], parts[1::2])]
    return parts[0]


def shards(query, key, value, gradient, hidden, doc_lengths, querya, queryb, valuea, valueb):
    n_ctx, n_dp = lax.axis_size("ctx"), lax.axis_size("dp")
    n_chips = n_ctx // 2
    q, k, v, g, x = query[0], key[0], value[0], gradient[0], hidden[0]
    rows, width = x.shape[0], x.shape[1] // 2
    rank = querya.shape[0]
    chip_rows = 2 * rows
    lanes = GROUP * chip_rows
    sds = jax.ShapeDtypeStruct

    def swap(a):
        return lax.ppermute(a, "ctx", [(i, i ^ 1) for i in range(n_ctx)])

    def up(a, step, first):
        chips = [(i, i + step) for i in range(n_chips - step) if i + step >= first]
        return lax.ppermute(a, "ctx", [(2 * i + c, 2 * j + c) for i, j in chips for c in (0, 1)])

    def down(a, step, first):
        chips = [(i, i - step) for i in range(step, n_chips) if i >= first]
        return lax.ppermute(a, "ctx", [(2 * i + c, 2 * j + c) for i, j in chips for c in (0, 1)])

    def across(a, bit):
        return lax.ppermute(a, "dp", [(i, i ^ bit) for i in range(n_dp)])

    def along(a, bit):
        return lax.ppermute(a, "ctx", [(i, i ^ (2 * bit)) for i in range(n_ctx)])

    kv_own, kv_send = call(split_kv, [sds((rows, 2 * KV_HALF), BF16)] * 2, (k, v))
    kv = [jnp.concatenate([kv_own, swap(kv_send)], axis=0)]
    if n_chips > 1:
        last = up(kv[0], n_chips - 1, n_chips - 1)
        for step in range(1, n_chips - 1):
            kv.append(up(kv[-1], 1, step))
        kv.append(last)

    pack, proj = call(
        split_rest,
        [sds((rows, 2 * Q_HALF + width), BF16), sds((2 * rank, rows), BF16)],
        (q, g, x, querya, valuea),
    )
    pack, proj_far = swap(pack), swap(proj)
    vp_own = jnp.concatenate([proj[rank:], proj_far[rank:]], axis=1)
    vp = [up(vp_own, step, step) for step in range(1, n_chips)]

    outs = (
        [sds((rows, Q_HALF), BF16)] * 2
        + [sds((rank, chip_rows), F32), sds((rank, Q_HALF), F32), sds((rank, KV_HALF), F32)]
        + [sds((chip_rows, 2 * KV_HALF), BF16)] * n_chips
        + [sds((rank, chip_rows), F32)] * n_chips
    )
    result = call(
        functools.partial(attention, n_chips, rank),
        outs,
        (doc_lengths, q, g, pack, proj, proj_far, queryb, valueb, *kv, *vp),
        scratch=[
            pltpu.VMEM((n_chips, chip_rows, 2 * KV_HALF), BF16),
            pltpu.VMEM((n_chips, rank, chip_rows), BF16),
            pltpu.VMEM((n_chips, chip_rows, 2 * KV_HALF), BF16),
            pltpu.VMEM((n_chips, rank, chip_rows), F32),
            pltpu.VMEM((n_chips, chip_rows, lanes), F32),
            pltpu.VMEM((n_chips, chip_rows, lanes), F32),
            pltpu.VMEM((chip_rows, lanes), BF16),
            pltpu.VMEM((chip_rows, lanes), BF16),
            pltpu.VMEM((CORE_HEADS, lanes, HEAD_WIDTH), BF16),
            pltpu.VMEM((CORE_HEADS, lanes, HEAD_WIDTH), BF16),
            pltpu.VMEM((HEAD_WIDTH, lanes), F32),
        ],
        flops=10 * CORE_HEADS * n_chips * chip_rows * lanes * HEAD_WIDTH,
        smem=(0,),
    )
    dq_own, dq_send, low, qbg, vbg = result[:5]
    dkv = result[5 : 5 + n_chips]
    vl = result[5 + n_chips :]

    value_low = vl[0]
    for step in range(1, n_chips):
        value_low = value_low + down(vl[step], step, step)
    lows = jnp.concatenate([low, value_low], axis=0)
    lows_far = swap(lows)

    if n_chips > 1:
        last = down(dkv[n_chips - 1], n_chips - 1, n_chips - 1)
        total = dkv[n_chips - 2]
        for step in range(n_chips - 2, 0, -1):
            total = down(total, 1, step).astype(F32) + dkv[step - 1].astype(F32)
            total = (total if step > 1 else total + last.astype(F32)).astype(BF16)
    else:
        total = dkv[0]
    dq_far = swap(dq_send)
    (query_grad,) = call(join_rows, [sds((rows, 2 * Q_HALF), BF16)], (dq_own, dq_far))
    dkv_far = swap(total[rows:])
    key_grad, value_grad = call(join_kv, [sds((rows, 2 * KV_HALF), BF16)] * 2, (total, dkv_far))

    used = 2 * width + Q_HALF + KV_HALF
    piece = -(-used // (128 * n_dp)) * 128
    pieces = call(
        functools.partial(adapters, n_dp, rank),
        [sds((rank, piece), BF16)] * n_dp,
        (lows, lows_far, x, pack, qbg, vbg),
        scratch=[pltpu.VMEM((rank, piece * n_dp), BF16)],
    )
    got = [pieces[0]] + [across(pieces[bit], bit) for bit in range(1, n_dp)]
    part = tree_sum([a.astype(F32) for a in got]).astype(BF16)
    got = [part] + [along(part, bit) for bit in range(1, n_chips)]
    part = tree_sum([a.astype(F32) for a in got]).astype(BF16)
    own = [part] + [across(part, bit) for bit in range(1, n_dp)]
    far = [swap(a) for a in own]
    qa_grad, qb_grad, va_grad, vb_grad = call(
        functools.partial(finish_adapters, n_dp, rank, width),
        [
            sds((rank, 2 * width), F32),
            sds((rank, 2 * Q_HALF), F32),
            sds((rank, 2 * width), F32),
            sds((rank, 2 * KV_HALF), F32),
        ],
        (*own, *far),
        scratch=[pltpu.VMEM((rank, piece * n_dp), F32)],
    )
    return (
        query_grad[None],
        key_grad[None],
        value_grad[None],
        qa_grad,
        qb_grad,
        va_grad,
        vb_grad,
    )


def solution(mesh):
    tokens = P("dp", "ctx", None)
    return jax.shard_map(
        shards,
        mesh=mesh,
        in_specs=(tokens,) * 5 + (P("dp", None),) + (P(),) * 4,
        out_specs=(tokens,) * 3 + (P(),) * 4,
        check_vma=False,
    )
```

```python
import functools

import jax
import jax.numpy as jnp
from jax import lax
from jax.experimental import pallas as pl
from jax.experimental.pallas import tpu as pltpu
from jax.sharding import PartitionSpec as P


QUERY_HEADS = 16
KEY_VALUE_HEADS = 4
HEAD_WIDTH = 128
NEG_FILL = -1e30
ADAPTER_SCALE = 2.0


F32 = jnp.float32
BF16 = jnp.bfloat16
VM = pl.BlockSpec(memory_space=pltpu.VMEM)
SM = pl.BlockSpec(memory_space=pltpu.SMEM)
AN = pl.BlockSpec(memory_space=pl.ANY)

CORE_HEADS = KEY_VALUE_HEADS // 2
GROUP = QUERY_HEADS // KEY_VALUE_HEADS
Q_HALF = QUERY_HEADS * HEAD_WIDTH // 2
KV_HALF = CORE_HEADS * HEAD_WIDTH


def dot_nn(a, b):
    return lax.dot_general(a, b, (((1,), (0,)), ((), ())), preferred_element_type=F32)


def dot_nt(a, b):
    return lax.dot_general(a, b, (((1,), (1,)), ((), ())), preferred_element_type=F32)


def dot_tn(a, b):
    return lax.dot_general(a, b, (((0,), (0,)), ((), ())), preferred_element_type=F32)


def half_of(ref, core, width):
    return ref[:, pl.ds(pl.multiple_of(core * width, 128), width)]


def call(body, outs, args, scratch=(), flops=0, smem=(), after=()):
    size = sum(a.size * a.dtype.itemsize for a in args)
    size += sum(o.size * o.dtype.itemsize for o in outs)
    return kernel_call(body, outs, args, scratch, flops, size, smem, after)


def kernel_call(body, outs, args, scratch, flops, size, smem, after):
    return pl.pallas_call(
        body,
        out_shape=outs,
        in_specs=[SM if i in smem else AN if i in after else VM for i in range(len(args))],
        out_specs=[VM] * len(outs),
        scratch_shapes=list(scratch),
        compiler_params=pltpu.CompilerParams(vmem_limit_bytes=60 << 20),
        cost_estimate=pl.CostEstimate(flops=flops, bytes_accessed=size, transcendentals=0),
    )(*args)


def split_kv(k_ref, v_ref, hidden_ref, qa_ref, va_ref, own_ref, send_ref):
    core = lax.axis_index("ctx") % 2
    rows = k_ref.shape[0]
    for i, ref in enumerate((k_ref, v_ref)):
        columns = slice(i * KV_HALF, (i + 1) * KV_HALF)
        own_ref[:rows, columns] = half_of(ref, core, KV_HALF)
        send_ref[:rows, columns] = half_of(ref, 1 - core, KV_HALF)
    at = 0
    for ref in (qa_ref, va_ref):
        down = dot_nt(ref[...], hidden_ref[...]).astype(BF16)
        for first in range(0, ref.shape[0], 8):
            own_ref[rows:, at : at + rows] = down[first : first + 8]
            send_ref[rows:, at : at + rows] = down[first : first + 8]
            at += rows


def split_rest(q_ref, g_ref, hidden_ref, _, pack_ref, send_ref):
    core = lax.axis_index("ctx") % 2
    pack_ref[:, :Q_HALF] = half_of(q_ref, 1 - core, Q_HALF)
    pack_ref[:, Q_HALF:] = half_of(g_ref, 1 - core, Q_HALF)
    send_ref[...] = half_of(hidden_ref, 1 - core, hidden_ref.shape[1] // 2)


def split_hidden(own_ref, far_ref, *outs):
    index = lax.axis_index("ctx")
    core, chip = index % 2, index // 2
    rows, width = far_ref.shape
    piece = width // 2
    for k in range(2):
        at = (chip % 2 ^ k) * piece
        outs[k][:rows] = own_ref[:, pl.ds(pl.multiple_of(core * width + at, 128), piece)]
        outs[k][rows:] = far_ref[:, pl.ds(pl.multiple_of(at, 128), piece)]


def attention(n_chips, rank, tail, *refs):
    lens_ref, q_ref, g_ref, pack_ref, qb_ref, vb_ref = refs[:6]
    kv_in = refs[6 : 6 + n_chips]
    refs = refs[6 + n_chips :]
    dq_own_ref, dq_send_ref = refs[:2]
    dkv_out = refs[2 : 2 + n_chips]
    message_out = refs[2 + n_chips : 2 + 2 * n_chips]
    kv, proj, dkv, vl, e_ref, dp_ref, stats, p_ref, ds_ref, qs, gs, dqt, ups, low_ref = refs[2 + 2 * n_chips :]
    rows = q_ref.shape[0]
    chip_rows = 2 * rows
    head_scale = HEAD_WIDTH ** (-0.5)
    index = lax.axis_index("ctx")
    core, chip = index % 2, index // 2
    block_rows = kv_in[0].shape[0] // 2

    for k in range(n_chips):
        for side in (0, 1):
            first = side * block_rows
            kv[k, side * rows : (side + 1) * rows] = kv_in[k][first : first + rows]
            for i in range(2 * rank // 8):
                proj[k, 8 * i : 8 * i + 8, side * rows : (side + 1) * rows] = kv_in[k][
                    first + rows : first + block_rows, i * rows : (i + 1) * rows
                ]
    for i in range(CORE_HEADS * GROUP):
        g, j = i // GROUP, i % GROUP
        at = pl.multiple_of(core * Q_HALF + i * HEAD_WIDTH, 128)
        top = slice(j * chip_rows, j * chip_rows + rows)
        low = slice(j * chip_rows + rows, (j + 1) * chip_rows)
        qs[g, top] = q_ref[:, pl.ds(at, HEAD_WIDTH)]
        qs[g, low] = pack_ref[:, i * HEAD_WIDTH : (i + 1) * HEAD_WIDTH]
        gs[g, top] = g_ref[:, pl.ds(at, HEAD_WIDTH)]
        gs[g, low] = pack_ref[:, Q_HALF + i * HEAD_WIDTH : Q_HALF + (i + 1) * HEAD_WIDTH]
    dkv[...] = jnp.zeros_like(dkv)
    vl[...] = jnp.zeros_like(vl)

    def local(t):
        return jnp.where(t < rows, core * rows + t, (1 - core) * rows + t - rows)

    row_pos = chip * chip_rows + local(lax.broadcasted_iota(jnp.int32, (1, chip_rows), 1))
    row_begin = jnp.zeros_like(row_pos)
    first_pos = chip * chip_rows
    first_begin = jnp.int32(0)
    begin = jnp.int32(0)
    for i in range(lens_ref.shape[1]):
        row_begin = jnp.where(row_pos >= begin, jnp.maximum(row_begin, begin), row_begin)
        first_begin = jnp.where(first_pos >= begin, jnp.maximum(first_begin, begin), first_begin)
        begin = begin + lens_ref[0, i]
    key_local = local(lax.broadcasted_iota(jnp.int32, (chip_rows, 1), 0))
    reach = (first_pos - first_begin + chip_rows - 1) // chip_rows + 1
    seen = jnp.minimum(reach, chip + 1)
    parts = [slice(j * chip_rows, (j + 1) * chip_rows) for j in range(GROUP)]

    def one_group(g, _):
        at_k = pl.multiple_of(g * HEAD_WIDTH, 128)
        at_v = pl.multiple_of(KV_HALF + g * HEAD_WIDTH, 128)

        def scores(k, carry):
            keys = kv[k, :, pl.ds(at_k, HEAD_WIDTH)]
            values = kv[k, :, pl.ds(at_v, HEAD_WIDTH)]
            key_pos = (chip - k) * chip_rows + key_local
            visible = (key_pos <= row_pos) & (key_pos >= row_begin)
            new = []
            for part, (top, total, delta) in zip(parts, carry):
                s = dot_nt(keys, qs[g, part]) * head_scale
                s = jnp.where(visible, s, NEG_FILL)
                own_top = jnp.max(s, axis=0, keepdims=True)
                e = jnp.exp(s - own_top)
                dp = dot_nt(values, gs[g, part])
                e_ref[k, :, part] = e
                dp_ref[k, :, part] = dp
                stats[k, :, part] = own_top
                new_top = jnp.maximum(top, own_top)
                old, now = jnp.exp(top - new_top), jnp.exp(own_top - new_top)
                total = total * old + jnp.sum(e, axis=0, keepdims=True) * now
                delta = delta * old + jnp.sum(e * dp, axis=0, keepdims=True) * now
                new.append((new_top, total, delta))
            return tuple(new)

        zero = jnp.zeros((1, chip_rows), F32)
        carry = ((jnp.full((1, chip_rows), NEG_FILL, F32), zero, zero),) * GROUP
        carry = lax.fori_loop(0, seen, scores, carry)
        inverse = [1.0 / total for _, total, _ in carry]
        delta = [d * i for (_, _, d), i in zip(carry, inverse)]
        dqt[...] = jnp.zeros_like(dqt)

        def gradients(k, _):
            keys = kv[k, :, pl.ds(at_k, HEAD_WIDTH)]
            for j, part in enumerate(parts):
                factor = jnp.exp(stats[k, :, part] - carry[j][0]) * inverse[j]
                p = e_ref[k, :, part] * factor
                p_ref[:, part] = p.astype(BF16)
                ds = p * (dp_ref[k, :, part] - delta[j]) * head_scale
                ds_ref[:, part] = ds.astype(BF16)
            ds = ds_ref[...]
            dv = dot_nn(p_ref[...], gs[g]).astype(BF16)
            dkv[k, :, pl.ds(at_k, HEAD_WIDTH)] = dot_nn(ds, qs[g]).astype(BF16)
            dkv[k, :, pl.ds(at_v, HEAD_WIDTH)] = dv
            dqt[...] += dot_tn(keys, ds)
            at_b = pl.multiple_of(core * KV_HALF + g * HEAD_WIDTH, 128)
            vl[chip - k] += dot_nt(vb_ref[:, pl.ds(at_b, HEAD_WIDTH)], dv)
            return 0

        lax.fori_loop(0, seen, gradients, 0)
        at_b = pl.multiple_of(core * Q_HALF + g * GROUP * HEAD_WIDTH, 128)
        for j, part in enumerate(parts):
            up = qb_ref[:, pl.ds(pl.multiple_of(at_b + j * HEAD_WIDTH, 128), HEAD_WIDTH)]
            low_ref[...] += dot_nn(up, dqt[:, part].astype(BF16))
            dq = jnp.transpose(dqt[:, part]).astype(BF16)
            at = pl.ds(pl.multiple_of((g * GROUP + j) * HEAD_WIDTH, 128), HEAD_WIDTH)
            dq_own_ref[:, at] = dq[:rows]
            dq_send_ref[:, at] = dq[rows:]
            ups[:, at] = dot_nn(proj[0, :rank], dq)
        return 0

    low_ref[...] = jnp.zeros_like(low_ref)
    ups[...] = jnp.zeros_like(ups)
    lax.fori_loop(0, CORE_HEADS, one_group, 0)
    total = jnp.zeros((rank, KV_HALF), F32)
    for k in range(n_chips):
        total = total + dot_nn(proj[k, rank:], dkv[k, :, KV_HALF:])
        dkv_out[k][...] = dkv[k]
    ups[:, Q_HALF : Q_HALF + KV_HALF] = total
    for k in range(n_chips):
        message_out[k][:, :chip_rows] = low_ref[...].astype(BF16)
        for i in range(2):
            message_out[k][:, (i + 1) * chip_rows : (i + 2) * chip_rows] = vl[chip ^ k ^ i].astype(BF16)
        at = pl.multiple_of((chip ^ k) * tail, 128)
        message_out[k][:, 3 * chip_rows :] = ups[:, pl.ds(at, tail)].astype(BF16)


def adapters(n_chips, rank, *refs):
    own, far = refs[:n_chips], refs[n_chips : 2 * n_chips]
    hidden = refs[2 * n_chips : 2 * n_chips + 2]
    out_ref = refs[-1]
    chip_rows, width = hidden[0].shape
    rows = chip_rows // 2
    query, value = jnp.zeros((rank, width), F32), jnp.zeros((rank, width), F32)
    for k in range(2):
        for first, other in ((0, rows), (rows, 0)):
            tokens = hidden[k][first : first + rows]
            low = own[k][:, first : first + rows].astype(F32) + far[k][:, other : other + rows].astype(F32)
            query += dot_nn(low.astype(BF16), tokens)
            at = (k + 1) * chip_rows
            low = sum(ref[:, at + first : at + first + rows].astype(F32) for ref in own)
            low += sum(ref[:, at + other : at + other + rows].astype(F32) for ref in far)
            value += dot_nn(low.astype(BF16), tokens)
    out_ref[:, :width] = (ADAPTER_SCALE * query).astype(BF16)
    out_ref[:, width : 2 * width] = (ADAPTER_SCALE * value).astype(BF16)
    tail = sum(ref[:, 3 * chip_rows :].astype(F32) for ref in own)
    out_ref[:, 2 * width :] = (ADAPTER_SCALE * tail).astype(BF16)


def finish_adapters(n_chips, tail, *refs):
    own, far = refs[:n_chips], refs[n_chips : 2 * n_chips]
    qa_ref, qb_ref, va_ref, vb_ref, buffer = refs[-5:]
    index = lax.axis_index("ctx")
    core, chip = index % 2, index // 2
    width = qa_ref.shape[1] // 4
    for half, pieces in ((core, own), (1 - core, far)):
        for side in (0, 1):
            total = tree_sum([ref[:, : 2 * width].astype(F32) for ref in pieces[side::2]])
            at = pl.ds(pl.multiple_of((2 * half + (chip % 2 ^ side)) * width, 128), width)
            qa_ref[:, at] = total[:, :width]
            va_ref[:, at] = total[:, width:]
        for k in range(n_chips):
            at = pl.ds(pl.multiple_of((chip ^ k) * tail, 128), tail)
            buffer[:, at] = pieces[k][:, 2 * width :].astype(F32)
        qb_ref[:, pl.ds(pl.multiple_of(half * Q_HALF, 128), Q_HALF)] = buffer[:, :Q_HALF]
        vb_ref[:, pl.ds(pl.multiple_of(half * KV_HALF, 128), KV_HALF)] = buffer[:, Q_HALF : Q_HALF + KV_HALF]


def join_rows(own_ref, far_ref, out_ref):
    core = lax.axis_index("ctx") % 2
    width = own_ref.shape[1]
    out_ref[:, pl.ds(pl.multiple_of(core * width, 128), width)] = own_ref[...]
    out_ref[:, pl.ds(pl.multiple_of((1 - core) * width, 128), width)] = far_ref[...]


def join_kv(own_ref, far_ref, dk_ref, dv_ref):
    core = lax.axis_index("ctx") % 2
    rows = far_ref.shape[0]
    for i, ref in enumerate((dk_ref, dv_ref)):
        columns = slice(i * KV_HALF, (i + 1) * KV_HALF)
        ref[:, pl.ds(pl.multiple_of(core * KV_HALF, 128), KV_HALF)] = own_ref[:rows, columns]
        ref[:, pl.ds(pl.multiple_of((1 - core) * KV_HALF, 128), KV_HALF)] = far_ref[:, columns]


def tree_sum(parts):
    while len(parts) > 1:
        parts = [a + b for a, b in zip(parts[::2], parts[1::2])]
    return parts[0]


def step(query, key, value, gradient, hidden, doc_lengths, querya, queryb, valuea, valueb):
    n_ctx, n_dp = lax.axis_size("ctx"), lax.axis_size("dp")
    n_chips = n_ctx // 2
    q, k, v, g, x = query[0], key[0], value[0], gradient[0], hidden[0]
    rows, width = x.shape[0], x.shape[1] // 2
    rank = querya.shape[0]
    chip_rows = 2 * rows
    lanes = GROUP * chip_rows
    sds = jax.ShapeDtypeStruct

    def swap(a):
        return lax.ppermute(a, "ctx", [(i, i ^ 1) for i in range(n_ctx)])

    def up(a, step):
        return lax.ppermute(a, "ctx", [(i, (i + 2 * step) % n_ctx) for i in range(n_ctx)])

    def down(a, step):
        return up(a, -step)

    def across(a, bit):
        return lax.ppermute(a, "dp", [(i, i ^ bit) for i in range(n_dp)])

    def along(a, bit):
        return lax.ppermute(a, "ctx", [(i, i ^ (2 * bit)) for i in range(n_ctx)])

    block = sds((rows + 2 * rank * rows // (2 * KV_HALF), 2 * KV_HALF), BF16)
    kv_own, kv_send = call(split_kv, [block] * 2, (k, v, x, querya, valuea))
    kv = [jnp.concatenate([kv_own, swap(kv_send)], axis=0)]
    if n_chips > 1:
        last = up(kv[0], n_chips - 1)
        for _ in range(1, n_chips - 1):
            kv.append(up(kv[-1], 1))
        kv.append(last)

    pack, hidden_far = call(
        split_rest,
        [sds((rows, 2 * Q_HALF), BF16), sds((rows, width), BF16)],
        (q, g, x, kv[0]),
        after=(3,),
    )
    pack, hidden_far = swap(pack), swap(hidden_far)
    hiddens = call(split_hidden, [sds((chip_rows, width // 2), BF16)] * 2, (x, hidden_far))
    hiddens = [hiddens[0], along(hiddens[1], 1)]

    tail = -(-(Q_HALF + KV_HALF) // (128 * n_chips)) * 128
    outs = (
        [sds((rows, Q_HALF), BF16)] * 2
        + [sds((chip_rows, 2 * KV_HALF), BF16)] * n_chips
        + [sds((rank, 3 * chip_rows + tail), BF16)] * n_chips
    )
    result = call(
        functools.partial(attention, n_chips, rank, tail),
        outs,
        (doc_lengths, q, g, pack, queryb, valueb, *kv),
        scratch=[
            pltpu.VMEM((n_chips, chip_rows, 2 * KV_HALF), BF16),
            pltpu.VMEM((n_chips, 2 * rank, chip_rows), BF16),
            pltpu.VMEM((n_chips, chip_rows, 2 * KV_HALF), BF16),
            pltpu.VMEM((n_chips, rank, chip_rows), F32),
            pltpu.VMEM((n_chips, chip_rows, lanes), F32),
            pltpu.VMEM((n_chips, chip_rows, lanes), F32),
            pltpu.VMEM((n_chips, 1, lanes), F32),
            pltpu.VMEM((chip_rows, lanes), BF16),
            pltpu.VMEM((chip_rows, lanes), BF16),
            pltpu.VMEM((CORE_HEADS, lanes, HEAD_WIDTH), BF16),
            pltpu.VMEM((CORE_HEADS, lanes, HEAD_WIDTH), BF16),
            pltpu.VMEM((HEAD_WIDTH, lanes), F32),
            pltpu.VMEM((rank, tail * n_chips), F32),
            pltpu.VMEM((rank, chip_rows), F32),
        ],
        flops=10 * CORE_HEADS * n_chips * chip_rows * lanes * HEAD_WIDTH,
        smem=(0,),
    )
    dq_own, dq_send = result[:2]
    dkv = result[2 : 2 + n_chips]
    messages = result[2 + n_chips :]

    own = [messages[0]] + [along(messages[bit], bit) for bit in range(1, n_chips)]
    far = [swap(a) for a in own]

    if n_chips > 1:
        last = down(dkv[n_chips - 1], n_chips - 1)
        total = dkv[n_chips - 2]
        for step in range(n_chips - 2, 0, -1):
            total = down(total, 1).astype(F32) + dkv[step - 1].astype(F32)
            total = (total if step > 1 else total + last.astype(F32)).astype(BF16)
    else:
        total = dkv[0]
    (query_grad,) = call(join_rows, [sds((rows, 2 * Q_HALF), BF16)], (dq_own, swap(dq_send)))
    dkv_far = swap(total[rows:])
    key_grad, value_grad = call(join_kv, [sds((rows, 2 * KV_HALF), BF16)] * 2, (total, dkv_far))

    (part,) = call(
        functools.partial(adapters, n_chips, rank),
        [sds((rank, width + tail), BF16)],
        (*own, *far, *hiddens, query_grad),
        after=(2 * n_chips + 2,),
    )
    got = [part] + [across(part, bit) for bit in range(1, n_dp)]
    part = tree_sum([a.astype(F32) for a in got]).astype(BF16)
    own = [part] + [along(part, bit) for bit in range(1, n_chips)]
    far = [swap(a) for a in own]
    qa_grad, qb_grad, va_grad, vb_grad = call(
        functools.partial(finish_adapters, n_chips, tail),
        [
            sds((rank, 2 * width), F32),
            sds((rank, 2 * Q_HALF), F32),
            sds((rank, 2 * width), F32),
            sds((rank, 2 * KV_HALF), F32),
        ],
        (*own, *far, key_grad, value_grad),
        scratch=[pltpu.VMEM((rank, tail * n_chips), F32)],
        after=(2 * n_chips, 2 * n_chips + 1),
    )
    return (
        query_grad[None],
        key_grad[None],
        value_grad[None],
        qa_grad,
        qb_grad,
        va_grad,
        vb_grad,
    )


def solution(mesh):
    tokens = P("dp", "ctx", None)
    return jax.shard_map(
        step,
        mesh=mesh,
        in_specs=(tokens,) * 5 + (P("dp", None),) + (P(),) * 4,
        out_specs=(tokens,) * 3 + (P(),) * 4,
        check_vma=False,
    )
```

```python
import functools
import math

import jax
import jax.numpy as jnp
from jax import lax
from jax.experimental import pallas as pl
from jax.experimental.pallas import tpu as pltpu
from jax.sharding import PartitionSpec as P


QUERY_HEADS = 16
KEY_VALUE_HEADS = 4
HEAD_WIDTH = 128
NEG_FILL = -1e30
ADAPTER_SCALE = 2.0
VMEM_MOST = 67043328


F32 = jnp.float32
BF16 = jnp.bfloat16
VM = pl.BlockSpec(memory_space=pltpu.VMEM)
SM = pl.BlockSpec(memory_space=pltpu.SMEM)
HB = pl.BlockSpec(memory_space=pltpu.HBM)

CORE_HEADS = KEY_VALUE_HEADS // 2
GROUP = QUERY_HEADS // KEY_VALUE_HEADS
Q_HALF = QUERY_HEADS * HEAD_WIDTH // 2
KV_HALF = CORE_HEADS * HEAD_WIDTH


def dot_nn(a, b):
    return lax.dot_general(a, b, (((1,), (0,)), ((), ())), preferred_element_type=F32)


def dot_nt(a, b):
    return lax.dot_general(a, b, (((1,), (1,)), ((), ())), preferred_element_type=F32)


def dot_tn(a, b):
    return lax.dot_general(a, b, (((0,), (0,)), ((), ())), preferred_element_type=F32)


def half_of(ref, core, width):
    return ref[:, pl.ds(pl.multiple_of(core * width, 128), width)]


def call(body, outs, args, scratch=(), flops=0, smem=(), hbm=(), limit=None):
    size = sum(a.size * a.dtype.itemsize for a in args)
    size += sum(o.size * o.dtype.itemsize for o in outs)
    held = size + sum(
        math.prod(m.shape) * jnp.dtype(m.dtype).itemsize
        for m in scratch
        if m.memory_space == pltpu.MemorySpace.VMEM
    )
    limit = min(limit or held + (4 << 20), VMEM_MOST)
    return kernel_call(body, outs, args, scratch, flops, size, limit, smem, hbm)


def kernel_call(body, outs, args, scratch, flops, size, limit, smem, hbm):
    return pl.pallas_call(
        body,
        out_shape=outs,
        in_specs=[SM if i in smem else HB if i in hbm else VM for i in range(len(args))],
        out_specs=[VM] * len(outs),
        scratch_shapes=list(scratch),
        compiler_params=pltpu.CompilerParams(vmem_limit_bytes=limit),
        cost_estimate=pl.CostEstimate(flops=flops, bytes_accessed=size, transcendentals=0),
    )(*args)


def split_kv(k_hbm, v_hbm, hidden_hbm, qa_hbm, va_hbm, own_ref, send_ref, hidden_ref, qa_ref, va_ref, sems):
    core = lax.axis_index("ctx") % 2
    rows = k_hbm.shape[0]
    copies = [(hidden_hbm, hidden_ref), (qa_hbm, qa_ref), (va_hbm, va_ref)]
    for i, source in enumerate((k_hbm, v_hbm)):
        columns = pl.ds(i * KV_HALF, KV_HALF)
        for half, target in ((core, own_ref), (1 - core, send_ref)):
            at = pl.ds(pl.multiple_of(half * KV_HALF, 128), KV_HALF)
            copies.append((source.at[:, at], target.at[pl.ds(0, rows), columns]))
    copies = [pltpu.make_async_copy(a, b, sems.at[i]) for i, (a, b) in enumerate(copies)]
    for copy in copies:
        copy.start()
    for copy in copies:
        copy.wait()
    at = 0
    for ref in (qa_ref, va_ref):
        down = dot_nt(ref[...], hidden_ref[...]).astype(BF16)
        for first in range(0, ref.shape[0], 8):
            own_ref[rows:, at : at + rows] = down[first : first + 8]
            send_ref[rows:, at : at + rows] = down[first : first + 8]
            at += rows


def split_rest(q_ref, g_ref, hidden_ref, pack_ref, send_ref):
    core = lax.axis_index("ctx") % 2
    pack_ref[:, :Q_HALF] = half_of(q_ref, 1 - core, Q_HALF)
    pack_ref[:, Q_HALF:] = half_of(g_ref, 1 - core, Q_HALF)
    send_ref[...] = half_of(hidden_ref, 1 - core, hidden_ref.shape[1] // 2)


def split_hidden(own_ref, far_ref, *outs):
    index = lax.axis_index("ctx")
    core, chip = index % 2, index // 2
    rows, width = far_ref.shape
    piece = width // 2
    for k in range(2):
        at = (chip % 2 ^ k) * piece
        outs[k][:rows] = own_ref[:, pl.ds(pl.multiple_of(core * width + at, 128), piece)]
        outs[k][rows:] = far_ref[:, pl.ds(pl.multiple_of(at, 128), piece)]


class Places:
    def __init__(self, lens_ref, rows):
        index = lax.axis_index("ctx")
        self.core, self.chip = index % 2, index // 2
        self.rows, self.chip_rows = rows, 2 * rows
        first_pos = self.chip * self.chip_rows
        self.row_pos = first_pos + self.local((1, self.chip_rows), 1)
        self.row_begin = jnp.zeros_like(self.row_pos)
        first_begin = jnp.int32(0)
        begin = jnp.int32(0)
        for i in range(lens_ref.shape[1]):
            inside = self.row_pos >= begin
            self.row_begin = jnp.where(inside, jnp.maximum(self.row_begin, begin), self.row_begin)
            first_begin = jnp.where(first_pos >= begin, jnp.maximum(first_begin, begin), first_begin)
            begin = begin + lens_ref[0, i]
        reach = (first_pos - first_begin + self.chip_rows - 1) // self.chip_rows + 1
        self.seen = jnp.minimum(reach, self.chip + 1)

    def local(self, shape, axis):
        t = lax.broadcasted_iota(jnp.int32, shape, axis)
        return jnp.where(t < self.rows, self.core * self.rows + t, (1 - self.core) * self.rows + t - self.rows)

    def visible(self, k):
        key_pos = (self.chip - k) * self.chip_rows + self.local((self.chip_rows, 1), 0)
        return (key_pos <= self.row_pos) & (key_pos >= self.row_begin)


def stack_heads(q_ref, g_ref, pack_ref, qs_ref, gs_ref):
    core = lax.axis_index("ctx") % 2
    rows = q_ref.shape[0]
    for i in range(CORE_HEADS * GROUP):
        g, j = i // GROUP, i % GROUP
        at = pl.ds(pl.multiple_of(core * Q_HALF + i * HEAD_WIDTH, 128), HEAD_WIDTH)
        first = 2 * j * rows
        for ref, out, base in ((q_ref, qs_ref, 0), (g_ref, gs_ref, Q_HALF)):
            out[g, first : first + rows] = ref[:, at]
            far = slice(base + i * HEAD_WIDTH, base + (i + 1) * HEAD_WIDTH)
            out[g, first + rows : first + 2 * rows] = pack_ref[:, far]


def key_rows(kv_ref, rows, columns):
    block_rows = kv_ref.shape[0] // 2
    halves = [kv_ref[first : first + rows, columns] for first in (0, block_rows)]
    return jnp.concatenate(halves, axis=0)


def head_parts(chip_rows):
    return [slice(j * chip_rows, (j + 1) * chip_rows) for j in range(GROUP)]


def chunk_scores(k, rows, lens_ref, kv_ref, *refs):
    if k == 0:
        stack_heads(*refs[:3], *refs[6:8])
        (e_ref, dp_ref, stats_ref), (qs_ref, gs_ref) = refs[3:6], refs[6:8]
    else:
        qs_ref, gs_ref, e_ref, dp_ref, stats_ref = refs
    places = Places(lens_ref, rows)
    head_scale = HEAD_WIDTH ** (-0.5)

    @pl.when(k < places.seen)
    def _():
        visible = places.visible(k)

        def one_group(g, _):
            keys = key_rows(kv_ref, rows, pl.ds(pl.multiple_of(g * HEAD_WIDTH, 128), HEAD_WIDTH))
            values = key_rows(kv_ref, rows, pl.ds(pl.multiple_of(KV_HALF + g * HEAD_WIDTH, 128), HEAD_WIDTH))
            for part in head_parts(2 * rows):
                s = dot_nt(keys, qs_ref[g, part]) * head_scale
                s = jnp.where(visible, s, NEG_FILL)
                top = jnp.max(s, axis=0, keepdims=True)
                e = jnp.exp(s - top)
                dp = dot_nt(values, gs_ref[g, part])
                e_ref[g, :, part] = e.astype(e_ref.dtype)
                dp_ref[g, :, part] = dp.astype(dp_ref.dtype)
                stats_ref[g, 0:1, part] = top
                stats_ref[g, 1:2, part] = jnp.sum(e, axis=0, keepdims=True)
                stats_ref[g, 2:3, part] = jnp.sum(e * dp, axis=0, keepdims=True)
            return 0

        lax.fori_loop(0, CORE_HEADS, one_group, 0)

    @pl.when(k >= places.seen)
    def _():
        stats_ref[:, 0:1] = jnp.full_like(stats_ref[:, 0:1], NEG_FILL)
        stats_ref[:, 1:3] = jnp.zeros_like(stats_ref[:, 1:3])


def gradients(n_chips, rank, rows, tail, *refs):
    lens_ref, qs, gs, qb_ref, vb_ref = refs[:5]
    refs = refs[5:]
    kv, e_in, dp_in, stats = (refs[i * n_chips : (i + 1) * n_chips] for i in range(4))
    refs = refs[4 * n_chips :]
    dq_own_ref, dq_send_ref = refs[:2]
    dkv = refs[2 : 2 + n_chips]
    message_out = refs[2 + n_chips : 2 + 2 * n_chips]
    proj, vl, p_ref, ds_ref, dqt, ups, low_ref = refs[2 + 2 * n_chips :]
    places = Places(lens_ref, rows)
    core, chip, chip_rows = places.core, places.chip, places.chip_rows
    head_scale = HEAD_WIDTH ** (-0.5)
    parts = head_parts(chip_rows)
    block_rows = kv[0].shape[0] // 2

    for k in range(n_chips):
        for side in (0, 1):
            first = side * block_rows + rows
            for i in range(2 * rank // 8):
                proj[k, 8 * i : 8 * i + 8, side * rows : (side + 1) * rows] = kv[k][
                    first : first + 8, i * rows : (i + 1) * rows
                ]
        if k:

            @pl.when(k >= places.seen)
            def _():
                dkv[k][...] = jnp.zeros_like(dkv[k])

    vl[...] = jnp.zeros_like(vl)
    low_ref[...] = jnp.zeros_like(low_ref)
    ups[...] = jnp.zeros_like(ups)

    def one_group(g, _):
        at_k = pl.ds(pl.multiple_of(g * HEAD_WIDTH, 128), HEAD_WIDTH)
        at_v = pl.ds(pl.multiple_of(KV_HALF + g * HEAD_WIDTH, 128), HEAD_WIDTH)
        top = functools.reduce(jnp.maximum, [ref[g, 0:1] for ref in stats])
        weight = [jnp.exp(ref[g, 0:1] - top) for ref in stats]
        inverse = 1.0 / sum(ref[g, 1:2] * w for ref, w in zip(stats, weight))
        delta = sum(ref[g, 2:3] * w for ref, w in zip(stats, weight)) * inverse
        dqt[...] = jnp.zeros_like(dqt)
        for k in range(n_chips):

            @pl.when(k < places.seen)
            def _():
                factor = weight[k] * inverse
                for part in parts:
                    p = e_in[k][g, :, part].astype(F32) * factor[:, part]
                    p_ref[:, part] = p.astype(BF16)
                    ds = p * (dp_in[k][g, :, part].astype(F32) - delta[:, part]) * head_scale
                    ds_ref[:, part] = ds.astype(BF16)
                ds = ds_ref[...]
                dv = dot_nn(p_ref[...], gs[g]).astype(BF16)
                dkv[k][:, at_k] = dot_nn(ds, qs[g]).astype(BF16)
                dkv[k][:, at_v] = dv
                dqt[...] += dot_tn(key_rows(kv[k], rows, at_k), ds)
                at_b = pl.multiple_of(core * KV_HALF + g * HEAD_WIDTH, 128)
                vl[chip - k] += dot_nt(vb_ref[:, pl.ds(at_b, HEAD_WIDTH)], dv)

        at_b = pl.multiple_of(core * Q_HALF + g * GROUP * HEAD_WIDTH, 128)
        for j, part in enumerate(parts):
            up = qb_ref[:, pl.ds(pl.multiple_of(at_b + j * HEAD_WIDTH, 128), HEAD_WIDTH)]
            low_ref[...] += dot_nn(up, dqt[:, part].astype(BF16))
            dq = jnp.transpose(dqt[:, part]).astype(BF16)
            at = pl.ds(pl.multiple_of((g * GROUP + j) * HEAD_WIDTH, 128), HEAD_WIDTH)
            dq_own_ref[:, at] = dq[:rows]
            dq_send_ref[:, at] = dq[rows:]
            ups[:, at] = dot_nn(proj[0, :rank], dq)
        return 0

    lax.fori_loop(0, CORE_HEADS, one_group, 0)
    for k in range(n_chips):

        @pl.when(k < places.seen)
        def _():
            ups[:, Q_HALF : Q_HALF + KV_HALF] += dot_nn(proj[k, rank:], dkv[k][:, KV_HALF:])

    for k in range(n_chips):
        message_out[k][:, :chip_rows] = low_ref[...].astype(BF16)
        for i in range(2):
            message_out[k][:, (i + 1) * chip_rows : (i + 2) * chip_rows] = vl[chip ^ k ^ i].astype(BF16)
        at = pl.multiple_of((chip ^ k) * tail, 128)
        message_out[k][:, 3 * chip_rows :] = ups[:, pl.ds(at, tail)].astype(BF16)


def adapters(n_chips, rank, *refs):
    own, far = refs[:n_chips], refs[n_chips : 2 * n_chips]
    hidden = refs[2 * n_chips : 2 * n_chips + 2]
    out_ref = refs[-1]
    chip_rows, width = hidden[0].shape
    rows = chip_rows // 2
    query, value = jnp.zeros((rank, width), F32), jnp.zeros((rank, width), F32)
    for k in range(2):
        for first, other in ((0, rows), (rows, 0)):
            tokens = hidden[k][first : first + rows]
            low = own[k][:, first : first + rows].astype(F32) + far[k][:, other : other + rows].astype(F32)
            query += dot_nn(low.astype(BF16), tokens)
            at = (k + 1) * chip_rows
            low = sum(ref[:, at + first : at + first + rows].astype(F32) for ref in own)
            low += sum(ref[:, at + other : at + other + rows].astype(F32) for ref in far)
            value += dot_nn(low.astype(BF16), tokens)
    out_ref[:, :width] = (ADAPTER_SCALE * query).astype(BF16)
    out_ref[:, width : 2 * width] = (ADAPTER_SCALE * value).astype(BF16)
    tail = sum(ref[:, 3 * chip_rows :].astype(F32) for ref in own)
    out_ref[:, 2 * width :] = (ADAPTER_SCALE * tail).astype(BF16)


def finish_adapters(n_chips, tail, *refs):
    own, far = refs[:n_chips], refs[n_chips : 2 * n_chips]
    qa_ref, qb_ref, va_ref, vb_ref, buffer = refs[-5:]
    index = lax.axis_index("ctx")
    core, chip = index % 2, index // 2
    width = qa_ref.shape[1] // 4
    for half, pieces in ((core, own), (1 - core, far)):
        for side in (0, 1):
            total = tree_sum([ref[:, : 2 * width].astype(F32) for ref in pieces[side::2]])
            at = pl.ds(pl.multiple_of((2 * half + (chip % 2 ^ side)) * width, 128), width)
            qa_ref[:, at] = total[:, :width]
            va_ref[:, at] = total[:, width:]
        for k in range(n_chips):
            at = pl.ds(pl.multiple_of((chip ^ k) * tail, 128), tail)
            buffer[:, at] = pieces[k][:, 2 * width :].astype(F32)
        qb_ref[:, pl.ds(pl.multiple_of(half * Q_HALF, 128), Q_HALF)] = buffer[:, :Q_HALF]
        vb_ref[:, pl.ds(pl.multiple_of(half * KV_HALF, 128), KV_HALF)] = buffer[:, Q_HALF : Q_HALF + KV_HALF]


def join_rows(own_ref, far_ref, out_ref):
    core = lax.axis_index("ctx") % 2
    width = own_ref.shape[1]
    out_ref[:, pl.ds(pl.multiple_of(core * width, 128), width)] = own_ref[...]
    out_ref[:, pl.ds(pl.multiple_of((1 - core) * width, 128), width)] = far_ref[...]


def join_kv(own_ref, far_ref, dk_ref, dv_ref):
    core = lax.axis_index("ctx") % 2
    rows = far_ref.shape[0]
    for i, ref in enumerate((dk_ref, dv_ref)):
        columns = slice(i * KV_HALF, (i + 1) * KV_HALF)
        ref[:, pl.ds(pl.multiple_of(core * KV_HALF, 128), KV_HALF)] = own_ref[:rows, columns]
        ref[:, pl.ds(pl.multiple_of((1 - core) * KV_HALF, 128), KV_HALF)] = far_ref[:, columns]


def tree_sum(parts):
    while len(parts) > 1:
        parts = [a + b for a, b in zip(parts[::2], parts[1::2])]
    return parts[0]


def step(query, key, value, gradient, hidden, doc_lengths, querya, queryb, valuea, valueb):
    n_ctx, n_dp = lax.axis_size("ctx"), lax.axis_size("dp")
    n_chips = n_ctx // 2
    q, k, v, g, x = query[0], key[0], value[0], gradient[0], hidden[0]
    rows, width = x.shape[0], x.shape[1] // 2
    rank = querya.shape[0]
    chip_rows = 2 * rows
    lanes = GROUP * chip_rows
    sds = jax.ShapeDtypeStruct

    def swap(a):
        return lax.ppermute(a, "ctx", [(i, i ^ 1) for i in range(n_ctx)])

    def up(a, step):
        return lax.ppermute(a, "ctx", [(i, (i + 2 * step) % n_ctx) for i in range(n_ctx)])

    def down(a, step):
        return up(a, -step)

    def across(a, bit):
        return lax.ppermute(a, "dp", [(i, i ^ bit) for i in range(n_dp)])

    def along(a, bit):
        return lax.ppermute(a, "ctx", [(i, i ^ (2 * bit)) for i in range(n_ctx)])

    block = sds((rows + 2 * rank * rows // (2 * KV_HALF), 2 * KV_HALF), BF16)
    kv_own, kv_send = call(
        split_kv,
        [block] * 2,
        (k, v, x, querya, valuea),
        scratch=[
            pltpu.VMEM(x.shape, BF16),
            pltpu.VMEM(querya.shape, BF16),
            pltpu.VMEM(valuea.shape, BF16),
            pltpu.SemaphoreType.DMA((7,)),
        ],
        hbm=range(5),
        limit=VMEM_MOST - (3 << 17),
    )
    kv = [jnp.concatenate([kv_own, swap(kv_send)], axis=0)]
    if n_chips > 1:
        last = up(kv[0], n_chips - 1)
        for _ in range(1, n_chips - 1):
            kv.append(up(kv[-1], 1))
        kv.append(last)

    pack, hidden_far = call(
        split_rest,
        [sds((rows, 2 * Q_HALF), BF16), sds((rows, width), BF16)],
        (q, g, x),
    )
    pack, hidden_far = swap(pack), swap(hidden_far)
    hiddens = call(split_hidden, [sds((chip_rows, width // 2), BF16)] * 2, (x, hidden_far))
    hiddens = [hiddens[0], along(hiddens[1], 1)]

    tail = -(-(Q_HALF + KV_HALF) // (128 * n_chips)) * 128
    tile = (CORE_HEADS, chip_rows, lanes)
    held = F32 if 8 * n_chips * math.prod(tile) <= 32 << 20 else BF16
    chunk = [sds(tile, held)] * 2 + [sds((CORE_HEADS, 8, lanes), F32)]
    stacked = sds((CORE_HEADS, lanes, HEAD_WIDTH), BF16)
    work = 2 * 2 * math.prod(tile) * HEAD_WIDTH
    chunks = [None] * n_chips
    *chunks[0], qs, gs = call(
        functools.partial(chunk_scores, 0, rows),
        chunk + [stacked] * 2,
        (doc_lengths, kv[0], q, g, pack),
        flops=work,
        smem=(0,),
    )
    for c in range(1, n_chips):
        chunks[c] = call(
            functools.partial(chunk_scores, c, rows), chunk, (doc_lengths, kv[c], qs, gs), flops=work, smem=(0,)
        )
    outs = (
        [sds((rows, Q_HALF), BF16)] * 2
        + [sds((chip_rows, 2 * KV_HALF), BF16)] * n_chips
        + [sds((rank, 3 * chip_rows + tail), BF16)] * n_chips
    )
    result = call(
        functools.partial(gradients, n_chips, rank, rows, tail),
        outs,
        (doc_lengths, qs, gs, queryb, valueb, *kv, *(c[i] for i in range(3) for c in chunks)),
        scratch=[
            pltpu.VMEM((n_chips, 2 * rank, chip_rows), BF16),
            pltpu.VMEM((n_chips, rank, chip_rows), F32),
            pltpu.VMEM((chip_rows, lanes), BF16),
            pltpu.VMEM((chip_rows, lanes), BF16),
            pltpu.VMEM((HEAD_WIDTH, lanes), F32),
            pltpu.VMEM((rank, tail * n_chips), F32),
            pltpu.VMEM((rank, chip_rows), F32),
        ],
        flops=3 * n_chips * work // 2,
        smem=(0,),
    )
    dq_own, dq_send = result[:2]
    dkv = result[2 : 2 + n_chips]
    messages = result[2 + n_chips :]

    own = [messages[0]] + [along(messages[bit], bit) for bit in range(1, n_chips)]
    far = [swap(a) for a in own]

    if n_chips > 1:
        last = down(dkv[n_chips - 1], n_chips - 1)
        total = dkv[n_chips - 2]
        for step in range(n_chips - 2, 0, -1):
            total = down(total, 1).astype(F32) + dkv[step - 1].astype(F32)
            total = (total if step > 1 else total + last.astype(F32)).astype(BF16)
    else:
        total = dkv[0]
    (query_grad,) = call(join_rows, [sds((rows, 2 * Q_HALF), BF16)], (dq_own, swap(dq_send)))
    dkv_far = swap(total[rows:])
    key_grad, value_grad = call(join_kv, [sds((rows, 2 * KV_HALF), BF16)] * 2, (total, dkv_far))

    (part,) = call(
        functools.partial(adapters, n_chips, rank),
        [sds((rank, width + tail), BF16)],
        (*own, *far, *hiddens),
    )
    got = [part] + [across(part, bit) for bit in range(1, n_dp)]
    part = tree_sum([a.astype(F32) for a in got]).astype(BF16)
    own = [part] + [along(part, bit) for bit in range(1, n_chips)]
    far = [swap(a) for a in own]
    qa_grad, qb_grad, va_grad, vb_grad = call(
        functools.partial(finish_adapters, n_chips, tail),
        [
            sds((rank, 2 * width), F32),
            sds((rank, 2 * Q_HALF), F32),
            sds((rank, 2 * width), F32),
            sds((rank, 2 * KV_HALF), F32),
        ],
        (*own, *far),
        scratch=[pltpu.VMEM((rank, tail * n_chips), F32)],
    )
    return (
        query_grad[None],
        key_grad[None],
        value_grad[None],
        qa_grad,
        qb_grad,
        va_grad,
        vb_grad,
    )


def solution(mesh):
    tokens = P("dp", "ctx", None)
    return jax.shard_map(
        step,
        mesh=mesh,
        in_specs=(tokens,) * 5 + (P("dp", None),) + (P(),) * 4,
        out_specs=(tokens,) * 3 + (P(),) * 4,
        check_vma=False,
    )
```

```python
import functools
import math

import jax
import jax.numpy as jnp
from jax import lax
from jax.experimental import pallas as pl
from jax.experimental.pallas import tpu as pltpu
from jax.sharding import PartitionSpec as P


QUERY_HEADS = 16
KEY_VALUE_HEADS = 4
HEAD_WIDTH = 128
NEG_FILL = -1e30
ADAPTER_SCALE = 2.0
VMEM_MOST = 67043328


F32 = jnp.float32
BF16 = jnp.bfloat16
VM = pl.BlockSpec(memory_space=pltpu.VMEM)
SM = pl.BlockSpec(memory_space=pltpu.SMEM)
HB = pl.BlockSpec(memory_space=pltpu.HBM)

CORE_HEADS = KEY_VALUE_HEADS // 2
GROUP = QUERY_HEADS // KEY_VALUE_HEADS
Q_HALF = QUERY_HEADS * HEAD_WIDTH // 2
KV_HALF = CORE_HEADS * HEAD_WIDTH


def dot_nn(a, b):
    return lax.dot_general(a, b, (((1,), (0,)), ((), ())), preferred_element_type=F32)


def dot_nt(a, b):
    return lax.dot_general(a, b, (((1,), (1,)), ((), ())), preferred_element_type=F32)


def dot_tn(a, b):
    return lax.dot_general(a, b, (((0,), (0,)), ((), ())), preferred_element_type=F32)


def half_of(ref, core, width):
    return ref[:, pl.ds(pl.multiple_of(core * width, 128), width)]


def call(body, outs, args, scratch=(), flops=0, smem=(), hbm=(), limit=None):
    size = sum(a.size * a.dtype.itemsize for a in args)
    size += sum(o.size * o.dtype.itemsize for o in outs)
    held = size + sum(
        math.prod(m.shape) * jnp.dtype(m.dtype).itemsize
        for m in scratch
        if m.memory_space == pltpu.MemorySpace.VMEM
    )
    limit = min(limit or held + (4 << 20), VMEM_MOST)
    return kernel_call(body, outs, args, scratch, flops, size, limit, smem, hbm)


def kernel_call(body, outs, args, scratch, flops, size, limit, smem, hbm):
    return pl.pallas_call(
        body,
        out_shape=outs,
        in_specs=[SM if i in smem else HB if i in hbm else VM for i in range(len(args))],
        out_specs=[VM] * len(outs),
        scratch_shapes=list(scratch),
        compiler_params=pltpu.CompilerParams(vmem_limit_bytes=limit),
        cost_estimate=pl.CostEstimate(flops=flops, bytes_accessed=size, transcendentals=0),
    )(*args)


def split_kv(k_hbm, v_hbm, hidden_hbm, qa_hbm, va_hbm, own_ref, send_ref, hidden_ref, qa_ref, va_ref, sems):
    core = lax.axis_index("ctx") % 2
    rows = k_hbm.shape[0]
    copies = [(hidden_hbm, hidden_ref), (qa_hbm, qa_ref), (va_hbm, va_ref)]
    for i, source in enumerate((k_hbm, v_hbm)):
        columns = pl.ds(i * KV_HALF, KV_HALF)
        for half, target in ((core, own_ref), (1 - core, send_ref)):
            at = pl.ds(pl.multiple_of(half * KV_HALF, 128), KV_HALF)
            copies.append((source.at[:, at], target.at[pl.ds(0, rows), columns]))
    copies = [pltpu.make_async_copy(a, b, sems.at[i]) for i, (a, b) in enumerate(copies)]
    for copy in copies:
        copy.start()
    for copy in copies:
        copy.wait()
    at = 0
    for ref in (qa_ref, va_ref):
        down = dot_nt(ref[...], hidden_ref[...]).astype(BF16)
        for first in range(0, ref.shape[0], 8):
            own_ref[rows:, at : at + rows] = down[first : first + 8]
            send_ref[rows:, at : at + rows] = down[first : first + 8]
            at += rows


def split_rest(q_ref, g_ref, hidden_ref, pack_ref, send_ref):
    core = lax.axis_index("ctx") % 2
    pack_ref[:, :Q_HALF] = half_of(q_ref, 1 - core, Q_HALF)
    pack_ref[:, Q_HALF:] = half_of(g_ref, 1 - core, Q_HALF)
    send_ref[...] = half_of(hidden_ref, 1 - core, hidden_ref.shape[1] // 2)


def split_hidden(own_ref, far_ref, *outs):
    index = lax.axis_index("ctx")
    core, chip = index % 2, index // 2
    rows, width = far_ref.shape
    piece = width // 2
    for k in range(2):
        at = (chip % 2 ^ k) * piece
        outs[k][:rows] = own_ref[:, pl.ds(pl.multiple_of(core * width + at, 128), piece)]
        outs[k][rows:] = far_ref[:, pl.ds(pl.multiple_of(at, 128), piece)]


class Places:
    def __init__(self, lens_ref, rows):
        index = lax.axis_index("ctx")
        self.core, self.chip = index % 2, index // 2
        self.rows, self.chip_rows = rows, 2 * rows
        first_pos = self.chip * self.chip_rows
        self.row_pos = first_pos + self.local((1, self.chip_rows), 1)
        self.row_begin = jnp.zeros_like(self.row_pos)
        first_begin = jnp.int32(0)
        begin = jnp.int32(0)
        for i in range(lens_ref.shape[1]):
            inside = self.row_pos >= begin
            self.row_begin = jnp.where(inside, jnp.maximum(self.row_begin, begin), self.row_begin)
            first_begin = jnp.where(first_pos >= begin, jnp.maximum(first_begin, begin), first_begin)
            begin = begin + lens_ref[0, i]
        reach = (first_pos - first_begin + self.chip_rows - 1) // self.chip_rows + 1
        self.seen = jnp.minimum(reach, self.chip + 1)

    def local(self, shape, axis):
        t = lax.broadcasted_iota(jnp.int32, shape, axis)
        return jnp.where(t < self.rows, self.core * self.rows + t, (1 - self.core) * self.rows + t - self.rows)

    def visible(self, k):
        key_pos = (self.chip - k) * self.chip_rows + self.local((self.chip_rows, 1), 0)
        return (key_pos <= self.row_pos) & (key_pos >= self.row_begin)


def stack_heads(q_ref, g_ref, pack_ref, qs_ref, gs_ref):
    core = lax.axis_index("ctx") % 2
    rows = q_ref.shape[0]
    for i in range(CORE_HEADS * GROUP):
        g, j = i // GROUP, i % GROUP
        at = pl.ds(pl.multiple_of(core * Q_HALF + i * HEAD_WIDTH, 128), HEAD_WIDTH)
        first = 2 * j * rows
        for ref, out, base in ((q_ref, qs_ref, 0), (g_ref, gs_ref, Q_HALF)):
            out[g, first : first + rows] = ref[:, at]
            far = slice(base + i * HEAD_WIDTH, base + (i + 1) * HEAD_WIDTH)
            out[g, first + rows : first + 2 * rows] = pack_ref[:, far]


def key_rows(halves, rows, columns):
    return jnp.concatenate([ref[:rows, columns] for ref in halves], axis=0)


def head_parts(chip_rows):
    return [slice(j * chip_rows, (j + 1) * chip_rows) for j in range(GROUP)]


def chunk_scores(k, rows, lens_ref, *refs):
    kv_ref, refs = refs[:2], refs[2:]
    if k == 0:
        stack_heads(*refs[:3], *refs[6:8])
        (e_ref, dp_ref, stats_ref), (qs_ref, gs_ref) = refs[3:6], refs[6:8]
    else:
        qs_ref, gs_ref, e_ref, dp_ref, stats_ref = refs
    places = Places(lens_ref, rows)
    scale = HEAD_WIDTH ** (-0.5) * math.log2(math.e)

    @pl.when(k < places.seen)
    def _():
        visible = places.visible(k)

        for g in range(CORE_HEADS):
            keys = key_rows(kv_ref, rows, slice(g * HEAD_WIDTH, (g + 1) * HEAD_WIDTH))
            values = key_rows(kv_ref, rows, slice(KV_HALF + g * HEAD_WIDTH, KV_HALF + (g + 1) * HEAD_WIDTH))
            for part in head_parts(2 * rows):
                s = dot_nt(keys, qs_ref[g, part]) * scale
                s = jnp.where(visible, s, NEG_FILL)
                top = jnp.max(s, axis=0, keepdims=True)
                e = jnp.exp2(s - top)
                dp = dot_nt(values, gs_ref[g, part])
                e_ref[g, :, part] = e.astype(e_ref.dtype)
                dp_ref[g, :, part] = dp.astype(dp_ref.dtype)
                stats_ref[g, 0:1, part] = top
                stats_ref[g, 1:2, part] = jnp.sum(e, axis=0, keepdims=True)
                stats_ref[g, 2:3, part] = jnp.sum(e * dp, axis=0, keepdims=True)

    @pl.when(k >= places.seen)
    def _():
        e_ref[...] = jnp.zeros_like(e_ref)
        dp_ref[...] = jnp.zeros_like(dp_ref)
        stats_ref[:, 0:1] = jnp.full_like(stats_ref[:, 0:1], NEG_FILL)
        stats_ref[:, 1:3] = jnp.zeros_like(stats_ref[:, 1:3])


def gradients(n_chips, rank, rows, tail, *refs):
    lens_ref, qs, gs, qb_ref, vb_ref = refs[:5]
    refs = refs[5:]
    kv = [refs[2 * i : 2 * i + 2] for i in range(n_chips)]
    refs = refs[2 * n_chips :]
    e_in, dp_in, stats = (refs[i * n_chips : (i + 1) * n_chips] for i in range(3))
    refs = refs[3 * n_chips :]
    dq_own_ref, dq_send_ref = refs[:2]
    dkv = refs[2 : 2 + n_chips]
    message_out = refs[2 + n_chips : 2 + 2 * n_chips]
    proj, vl, p_ref, ds_ref, dqt, ups, low_ref = refs[2 + 2 * n_chips :]
    places = Places(lens_ref, rows)
    core, chip, chip_rows = places.core, places.chip, places.chip_rows
    head_scale = HEAD_WIDTH ** (-0.5)
    parts = head_parts(chip_rows)

    for k in range(n_chips):
        for side in (0, 1):
            for i in range(2 * rank // 8):
                proj[k, 8 * i : 8 * i + 8, side * rows : (side + 1) * rows] = kv[k][side][
                    rows:, i * rows : (i + 1) * rows
                ]
    vl[...] = jnp.zeros_like(vl)
    low_ref[...] = jnp.zeros_like(low_ref)
    ups[...] = jnp.zeros_like(ups)

    def one_group(g, _):
        at_k = pl.ds(pl.multiple_of(g * HEAD_WIDTH, 128), HEAD_WIDTH)
        at_v = pl.ds(pl.multiple_of(KV_HALF + g * HEAD_WIDTH, 128), HEAD_WIDTH)
        top = functools.reduce(jnp.maximum, [ref[g, 0:1] for ref in stats])
        weight = [jnp.exp2(ref[g, 0:1] - top) for ref in stats]
        inverse = 1.0 / sum(ref[g, 1:2] * w for ref, w in zip(stats, weight))
        delta = sum(ref[g, 2:3] * w for ref, w in zip(stats, weight)) * inverse
        at_b = pl.multiple_of(core * KV_HALF + g * HEAD_WIDTH, 128)
        for k in range(n_chips):
            factor = weight[k] * inverse
            slot = k % 2
            for part in parts:
                p = e_in[k][g, :, part].astype(F32) * factor[:, part]
                p_ref[slot, :, part] = p.astype(BF16)
                ds = p * (dp_in[k][g, :, part].astype(F32) - delta[:, part])
                ds_ref[slot, :, part] = ds.astype(BF16)
            ds = ds_ref[slot]
            dv = dot_nn(p_ref[slot], gs[g]).astype(BF16)
            dkv[k][:, at_k] = (dot_nn(ds, qs[g]) * head_scale).astype(BF16)
            dkv[k][:, at_v] = dv
            if k == 0:
                dqt[...] = dot_tn(key_rows(kv[k], rows, at_k), ds)
            else:
                dqt[...] += dot_tn(key_rows(kv[k], rows, at_k), ds)
            low = dot_nt(vb_ref[:, pl.ds(at_b, HEAD_WIDTH)], dv)
            vl[(chip - k + n_chips) % n_chips] += low
        dqt[...] *= head_scale

        at_b = pl.multiple_of(core * Q_HALF + g * GROUP * HEAD_WIDTH, 128)
        for j, part in enumerate(parts):
            up = qb_ref[:, pl.ds(pl.multiple_of(at_b + j * HEAD_WIDTH, 128), HEAD_WIDTH)]
            low_ref[...] += dot_nn(up, dqt[:, part].astype(BF16))
            dq = jnp.transpose(dqt[:, part]).astype(BF16)
            at = pl.ds(pl.multiple_of((g * GROUP + j) * HEAD_WIDTH, 128), HEAD_WIDTH)
            dq_own_ref[:, at] = dq[:rows]
            dq_send_ref[:, at] = dq[rows:]
            ups[:, at] = dot_nn(proj[0, :rank], dq)
        return 0

    lax.fori_loop(0, CORE_HEADS, one_group, 0)
    total = jnp.zeros((rank, KV_HALF), F32)
    for k in range(n_chips):
        total = total + dot_nn(proj[k, rank:], dkv[k][:, KV_HALF:])
    ups[:, Q_HALF : Q_HALF + KV_HALF] = total

    for k in range(n_chips):
        message_out[k][:, :chip_rows] = low_ref[...].astype(BF16)
        for i in range(2):
            message_out[k][:, (i + 1) * chip_rows : (i + 2) * chip_rows] = vl[chip ^ k ^ i].astype(BF16)
        at = pl.multiple_of((chip ^ k) * tail, 128)
        message_out[k][:, 3 * chip_rows :] = ups[:, pl.ds(at, tail)].astype(BF16)


def adapters(n_chips, rank, *refs):
    own, far = refs[:n_chips], refs[n_chips : 2 * n_chips]
    hidden = refs[2 * n_chips : 2 * n_chips + 2]
    out_ref = refs[-1]
    chip_rows, width = hidden[0].shape
    rows = chip_rows // 2
    query, value = jnp.zeros((rank, width), F32), jnp.zeros((rank, width), F32)
    for k in range(2):
        for first, other in ((0, rows), (rows, 0)):
            tokens = hidden[k][first : first + rows]
            low = own[k][:, first : first + rows].astype(F32) + far[k][:, other : other + rows].astype(F32)
            query += dot_nn(low.astype(BF16), tokens)
            at = (k + 1) * chip_rows
            low = sum(ref[:, at + first : at + first + rows].astype(F32) for ref in own)
            low += sum(ref[:, at + other : at + other + rows].astype(F32) for ref in far)
            value += dot_nn(low.astype(BF16), tokens)
    out_ref[:, :width] = (ADAPTER_SCALE * query).astype(BF16)
    out_ref[:, width : 2 * width] = (ADAPTER_SCALE * value).astype(BF16)
    tail = sum(ref[:, 3 * chip_rows :].astype(F32) for ref in own)
    out_ref[:, 2 * width :] = (ADAPTER_SCALE * tail).astype(BF16)


def finish_adapters(n_chips, tail, *refs):
    own, far = refs[:n_chips], refs[n_chips : 2 * n_chips]
    qa_ref, qb_ref, va_ref, vb_ref, buffer = refs[-5:]
    index = lax.axis_index("ctx")
    core, chip = index % 2, index // 2
    width = qa_ref.shape[1] // 4
    for half, pieces in ((core, own), (1 - core, far)):
        for side in (0, 1):
            total = tree_sum([ref[:, : 2 * width].astype(F32) for ref in pieces[side::2]])
            at = pl.ds(pl.multiple_of((2 * half + (chip % 2 ^ side)) * width, 128), width)
            qa_ref[:, at] = total[:, :width]
            va_ref[:, at] = total[:, width:]
        for k in range(n_chips):
            at = pl.ds(pl.multiple_of((chip ^ k) * tail, 128), tail)
            buffer[:, at] = pieces[k][:, 2 * width :].astype(F32)
        qb_ref[:, pl.ds(pl.multiple_of(half * Q_HALF, 128), Q_HALF)] = buffer[:, :Q_HALF]
        vb_ref[:, pl.ds(pl.multiple_of(half * KV_HALF, 128), KV_HALF)] = buffer[:, Q_HALF : Q_HALF + KV_HALF]


def join_rows(own_ref, far_ref, out_ref):
    core = lax.axis_index("ctx") % 2
    width = own_ref.shape[1]
    out_ref[:, pl.ds(pl.multiple_of(core * width, 128), width)] = own_ref[...]
    out_ref[:, pl.ds(pl.multiple_of((1 - core) * width, 128), width)] = far_ref[...]


def join_kv(own_ref, far_ref, dk_ref, dv_ref):
    core = lax.axis_index("ctx") % 2
    rows = far_ref.shape[0]
    for i, ref in enumerate((dk_ref, dv_ref)):
        columns = slice(i * KV_HALF, (i + 1) * KV_HALF)
        ref[:, pl.ds(pl.multiple_of(core * KV_HALF, 128), KV_HALF)] = own_ref[:rows, columns]
        ref[:, pl.ds(pl.multiple_of((1 - core) * KV_HALF, 128), KV_HALF)] = far_ref[:, columns]


def tree_sum(parts):
    while len(parts) > 1:
        parts = [a + b for a, b in zip(parts[::2], parts[1::2])]
    return parts[0]


def step(query, key, value, gradient, hidden, doc_lengths, querya, queryb, valuea, valueb):
    n_ctx, n_dp = lax.axis_size("ctx"), lax.axis_size("dp")
    n_chips = n_ctx // 2
    q, k, v, g, x = query[0], key[0], value[0], gradient[0], hidden[0]
    rows, width = x.shape[0], x.shape[1] // 2
    rank = querya.shape[0]
    chip_rows = 2 * rows
    lanes = GROUP * chip_rows
    sds = jax.ShapeDtypeStruct

    def swap(a):
        return lax.ppermute(a, "ctx", [(i, i ^ 1) for i in range(n_ctx)])

    def up(a, step):
        return lax.ppermute(a, "ctx", [(i, (i + 2 * step) % n_ctx) for i in range(n_ctx)])

    def down(a, step):
        return up(a, -step)

    def across(a, bit):
        return lax.ppermute(a, "dp", [(i, i ^ bit) for i in range(n_dp)])

    def along(a, bit):
        return lax.ppermute(a, "ctx", [(i, i ^ (2 * bit)) for i in range(n_ctx)])

    block = sds((rows + 2 * rank * rows // (2 * KV_HALF), 2 * KV_HALF), BF16)
    kv_own, kv_send = call(
        split_kv,
        [block] * 2,
        (k, v, x, querya, valuea),
        scratch=[
            pltpu.VMEM(x.shape, BF16),
            pltpu.VMEM(querya.shape, BF16),
            pltpu.VMEM(valuea.shape, BF16),
            pltpu.SemaphoreType.DMA((7,)),
        ],
        hbm=range(5),
        limit=VMEM_MOST - (3 << 17),
    )
    kv = []
    for block in (kv_own, swap(kv_send)):
        chain = [block]
        if n_chips > 1:
            last = up(block, n_chips - 1)
            for _ in range(1, n_chips - 1):
                chain.append(up(chain[-1], 1))
            chain.append(last)
        kv.append(chain)
    kv = list(zip(*kv))

    pack, hidden_far = call(
        split_rest,
        [sds((rows, 2 * Q_HALF), BF16), sds((rows, width), BF16)],
        (q, g, x),
    )
    pack, hidden_far = swap(pack), swap(hidden_far)
    hiddens = call(split_hidden, [sds((chip_rows, width // 2), BF16)] * 2, (x, hidden_far))
    hiddens = [hiddens[0], along(hiddens[1], 1)]

    tail = -(-(Q_HALF + KV_HALF) // (128 * n_chips)) * 128
    tile = (CORE_HEADS, chip_rows, lanes)
    held = F32 if 8 * n_chips * math.prod(tile) <= 32 << 20 else BF16
    chunk = [sds(tile, held)] * 2 + [sds((CORE_HEADS, 8, lanes), F32)]
    stacked = sds((CORE_HEADS, lanes, HEAD_WIDTH), BF16)
    work = 2 * 2 * math.prod(tile) * HEAD_WIDTH
    chunks = [None] * n_chips
    *chunks[0], qs, gs = call(
        functools.partial(chunk_scores, 0, rows),
        chunk + [stacked] * 2,
        (doc_lengths, *kv[0], q, g, pack),
        flops=work,
        smem=(0,),
    )
    for c in range(1, n_chips):
        chunks[c] = call(
            functools.partial(chunk_scores, c, rows), chunk, (doc_lengths, *kv[c], qs, gs), flops=work, smem=(0,)
        )
    outs = (
        [sds((rows, Q_HALF), BF16)] * 2
        + [sds((chip_rows, 2 * KV_HALF), BF16)] * n_chips
        + [sds((rank, 3 * chip_rows + tail), BF16)] * n_chips
    )
    result = call(
        functools.partial(gradients, n_chips, rank, rows, tail),
        outs,
        (doc_lengths, qs, gs, queryb, valueb, *sum(kv, ()), *(c[i] for i in range(3) for c in chunks)),
        scratch=[
            pltpu.VMEM((n_chips, 2 * rank, chip_rows), BF16),
            pltpu.VMEM((n_chips, rank, chip_rows), F32),
            pltpu.VMEM((2, chip_rows, lanes), BF16),
            pltpu.VMEM((2, chip_rows, lanes), BF16),
            pltpu.VMEM((HEAD_WIDTH, lanes), F32),
            pltpu.VMEM((rank, tail * n_chips), F32),
            pltpu.VMEM((rank, chip_rows), F32),
        ],
        flops=3 * n_chips * work // 2,
        smem=(0,),
    )
    dq_own, dq_send = result[:2]
    dkv = result[2 : 2 + n_chips]
    messages = result[2 + n_chips :]

    own = [messages[0]] + [along(messages[bit], bit) for bit in range(1, n_chips)]
    far = [swap(a) for a in own]

    if n_chips > 1:
        last = down(dkv[n_chips - 1], n_chips - 1)
        total = dkv[n_chips - 2]
        for step in range(n_chips - 2, 0, -1):
            total = down(total, 1).astype(F32) + dkv[step - 1].astype(F32)
            total = (total if step > 1 else total + last.astype(F32)).astype(BF16)
    else:
        total = dkv[0]
    (query_grad,) = call(join_rows, [sds((rows, 2 * Q_HALF), BF16)], (dq_own, swap(dq_send)))
    dkv_far = swap(total[rows:])
    key_grad, value_grad = call(join_kv, [sds((rows, 2 * KV_HALF), BF16)] * 2, (total, dkv_far))

    (part,) = call(
        functools.partial(adapters, n_chips, rank),
        [sds((rank, width + tail), BF16)],
        (*own, *far, *hiddens),
    )
    got = [part] + [across(part, bit) for bit in range(1, n_dp)]
    part = tree_sum([a.astype(F32) for a in got]).astype(BF16)
    own = [part] + [along(part, bit) for bit in range(1, n_chips)]
    far = [swap(a) for a in own]
    qa_grad, qb_grad, va_grad, vb_grad = call(
        functools.partial(finish_adapters, n_chips, tail),
        [
            sds((rank, 2 * width), F32),
            sds((rank, 2 * Q_HALF), F32),
            sds((rank, 2 * width), F32),
            sds((rank, 2 * KV_HALF), F32),
        ],
        (*own, *far),
        scratch=[pltpu.VMEM((rank, tail * n_chips), F32)],
    )
    return (
        query_grad[None],
        key_grad[None],
        value_grad[None],
        qa_grad,
        qb_grad,
        va_grad,
        vb_grad,
    )


def solution(mesh):
    tokens = P("dp", "ctx", None)
    return jax.shard_map(
        step,
        mesh=mesh,
        in_specs=(tokens,) * 5 + (P("dp", None),) + (P(),) * 4,
        out_specs=(tokens,) * 3 + (P(),) * 4,
        check_vma=False,
    )
```

```python
import functools
import math

import jax
import jax.numpy as jnp
from jax import lax
from jax.experimental import pallas as pl
from jax.experimental.pallas import tpu as pltpu
from jax.sharding import PartitionSpec as P


QUERY_HEADS = 16
KEY_VALUE_HEADS = 4
HEAD_WIDTH = 128
NEG_FILL = -1e30
ADAPTER_SCALE = 2.0
VMEM_MOST = 67043328


F32 = jnp.float32
BF16 = jnp.bfloat16
VM = pl.BlockSpec(memory_space=pltpu.VMEM)
SM = pl.BlockSpec(memory_space=pltpu.SMEM)
HB = pl.BlockSpec(memory_space=pltpu.HBM)

CORE_HEADS = KEY_VALUE_HEADS // 2
GROUP = QUERY_HEADS // KEY_VALUE_HEADS
Q_HALF = QUERY_HEADS * HEAD_WIDTH // 2
KV_HALF = CORE_HEADS * HEAD_WIDTH


def dot_nn(a, b):
    return lax.dot_general(a, b, (((1,), (0,)), ((), ())), preferred_element_type=F32)


def dot_nt(a, b):
    return lax.dot_general(a, b, (((1,), (1,)), ((), ())), preferred_element_type=F32)


def dot_tn(a, b):
    return lax.dot_general(a, b, (((0,), (0,)), ((), ())), preferred_element_type=F32)


def half_of(ref, core, width):
    return ref[:, pl.ds(pl.multiple_of(core * width, 128), width)]


def call(body, outs, args, scratch=(), flops=0, smem=(), hbm=(), limit=None):
    size = sum(a.size * a.dtype.itemsize for a in args)
    size += sum(o.size * o.dtype.itemsize for o in outs)
    held = size + sum(
        math.prod(m.shape) * jnp.dtype(m.dtype).itemsize
        for m in scratch
        if m.memory_space == pltpu.MemorySpace.VMEM
    )
    limit = min(limit or held + (4 << 20), VMEM_MOST)
    return kernel_call(body, outs, args, scratch, flops, size, limit, smem, hbm)


def kernel_call(body, outs, args, scratch, flops, size, limit, smem, hbm):
    return pl.pallas_call(
        body,
        out_shape=outs,
        in_specs=[SM if i in smem else HB if i in hbm else VM for i in range(len(args))],
        out_specs=[VM] * len(outs),
        scratch_shapes=list(scratch),
        compiler_params=pltpu.CompilerParams(vmem_limit_bytes=limit),
        cost_estimate=pl.CostEstimate(flops=flops, bytes_accessed=size, transcendentals=0),
    )(*args)


def split_kv(k_hbm, v_hbm, hidden_hbm, qa_hbm, va_hbm, own_ref, send_ref, hidden_ref, maps_ref, sems):
    core = lax.axis_index("ctx") % 2
    rows = k_hbm.shape[0]
    rank, width = qa_hbm.shape
    piece = width // 4
    moves = [(qa_hbm, maps_ref.at[pl.ds(0, rank)]), (va_hbm, maps_ref.at[pl.ds(rank, rank)])]
    for i in range(4):
        columns = pl.ds(i * piece, piece)
        moves.append((hidden_hbm.at[:, columns], hidden_ref.at[:, columns]))
    for i, source in enumerate((k_hbm, v_hbm)):
        columns = pl.ds(i * KV_HALF, KV_HALF)
        for half, target in ((core, own_ref), (1 - core, send_ref)):
            at = pl.ds(pl.multiple_of(half * KV_HALF, 128), KV_HALF)
            moves.append((source.at[:, at], target.at[pl.ds(0, rows), columns]))
    copies = [pltpu.make_async_copy(a, b, sems.at[i]) for i, (a, b) in enumerate(moves)]
    for copy in copies:
        copy.start()
    for copy in copies[:2]:
        copy.wait()
    down = jnp.zeros((2 * rank, rows), F32)
    for i in range(4):
        copies[2 + i].wait()
        columns = slice(i * piece, (i + 1) * piece)
        down += dot_nt(maps_ref[:, columns], hidden_ref[:, columns])
    down = down.astype(BF16)
    for i in range(2 * rank // 8):
        own_ref[rows:, i * rows : (i + 1) * rows] = down[8 * i : 8 * i + 8]
        send_ref[rows:, i * rows : (i + 1) * rows] = down[8 * i : 8 * i + 8]
    for copy in copies[6:]:
        copy.wait()


def split_rest(q_ref, g_ref, hidden_ref, pack_ref, send_ref):
    core = lax.axis_index("ctx") % 2
    pack_ref[:, :Q_HALF] = half_of(q_ref, 1 - core, Q_HALF)
    pack_ref[:, Q_HALF:] = half_of(g_ref, 1 - core, Q_HALF)
    send_ref[...] = half_of(hidden_ref, 1 - core, hidden_ref.shape[1] // 2)


def split_hidden(own_ref, far_ref, *outs):
    index = lax.axis_index("ctx")
    core, chip = index % 2, index // 2
    rows, width = far_ref.shape
    piece = width // 2
    for k in range(2):
        at = (chip % 2 ^ k) * piece
        outs[k][:rows] = own_ref[:, pl.ds(pl.multiple_of(core * width + at, 128), piece)]
        outs[k][rows:] = far_ref[:, pl.ds(pl.multiple_of(at, 128), piece)]


class Places:
    def __init__(self, lens_ref, rows):
        index = lax.axis_index("ctx")
        self.core, self.chip = index % 2, index // 2
        self.rows, self.chip_rows = rows, 2 * rows
        first_pos = self.chip * self.chip_rows
        self.row_pos = first_pos + self.local((1, self.chip_rows), 1)
        self.row_begin = jnp.zeros_like(self.row_pos)
        first_begin = jnp.int32(0)
        begin = jnp.int32(0)
        for i in range(lens_ref.shape[1]):
            inside = self.row_pos >= begin
            self.row_begin = jnp.where(inside, jnp.maximum(self.row_begin, begin), self.row_begin)
            first_begin = jnp.where(first_pos >= begin, jnp.maximum(first_begin, begin), first_begin)
            begin = begin + lens_ref[0, i]
        reach = (first_pos - first_begin + self.chip_rows - 1) // self.chip_rows + 1
        self.seen = jnp.minimum(reach, self.chip + 1)

    def local(self, shape, axis):
        t = lax.broadcasted_iota(jnp.int32, shape, axis)
        return jnp.where(t < self.rows, self.core * self.rows + t, (1 - self.core) * self.rows + t - self.rows)

    def visible(self, k):
        key_pos = (self.chip - k) * self.chip_rows + self.local((self.chip_rows, 1), 0)
        return (key_pos <= self.row_pos) & (key_pos >= self.row_begin)


def stack_heads(q_ref, g_ref, pack_ref, qs_ref, gs_ref):
    core = lax.axis_index("ctx") % 2
    rows = q_ref.shape[0]
    for i in range(CORE_HEADS * GROUP):
        g, j = i // GROUP, i % GROUP
        at = pl.ds(pl.multiple_of(core * Q_HALF + i * HEAD_WIDTH, 128), HEAD_WIDTH)
        first = 2 * j * rows
        for ref, out, base in ((q_ref, qs_ref, 0), (g_ref, gs_ref, Q_HALF)):
            out[g, first : first + rows] = ref[:, at]
            far = slice(base + i * HEAD_WIDTH, base + (i + 1) * HEAD_WIDTH)
            out[g, first + rows : first + 2 * rows] = pack_ref[:, far]


def key_rows(halves, rows, columns):
    return jnp.concatenate([ref[:rows, columns] for ref in halves], axis=0)


def head_parts(chip_rows):
    return [slice(j * chip_rows, (j + 1) * chip_rows) for j in range(GROUP)]


def chunk_scores(k, rows, lens_ref, *refs):
    kv_ref, refs = refs[:2], refs[2:]
    if k == 0:
        stack_heads(*refs[:3], *refs[6:8])
        (e_ref, dp_ref, stats_ref), (qs_ref, gs_ref) = refs[3:6], refs[6:8]
    else:
        qs_ref, gs_ref, e_ref, dp_ref, stats_ref = refs
    places = Places(lens_ref, rows)
    scale = HEAD_WIDTH ** (-0.5) * math.log2(math.e)

    @pl.when(k < places.seen)
    def _():
        visible = places.visible(k)

        for g in range(CORE_HEADS):
            keys = key_rows(kv_ref, rows, slice(g * HEAD_WIDTH, (g + 1) * HEAD_WIDTH))
            values = key_rows(kv_ref, rows, slice(KV_HALF + g * HEAD_WIDTH, KV_HALF + (g + 1) * HEAD_WIDTH))
            for part in head_parts(2 * rows):
                s = dot_nt(keys, qs_ref[g, part]) * scale
                s = jnp.where(visible, s, NEG_FILL)
                top = jnp.max(s, axis=0, keepdims=True)
                e = jnp.exp2(s - top)
                dp = dot_nt(values, gs_ref[g, part])
                e_ref[g, :, part] = e.astype(e_ref.dtype)
                dp_ref[g, :, part] = dp.astype(dp_ref.dtype)
                stats_ref[g, 0:1, part] = top
                stats_ref[g, 1:2, part] = jnp.sum(e, axis=0, keepdims=True)
                stats_ref[g, 2:3, part] = jnp.sum(e * dp, axis=0, keepdims=True)

    @pl.when(k >= places.seen)
    def _():
        e_ref[...] = jnp.zeros_like(e_ref)
        dp_ref[...] = jnp.zeros_like(dp_ref)
        stats_ref[:, 0:1] = jnp.full_like(stats_ref[:, 0:1], NEG_FILL)
        stats_ref[:, 1:3] = jnp.zeros_like(stats_ref[:, 1:3])


def gradients(n_chips, rank, rows, tail, *refs):
    lens_ref, qs, gs, qb_ref, vb_ref = refs[:5]
    refs = refs[5:]
    kv = [refs[2 * i : 2 * i + 2] for i in range(n_chips)]
    refs = refs[2 * n_chips :]
    e_in, dp_in, stats = (refs[i * n_chips : (i + 1) * n_chips] for i in range(3))
    refs = refs[3 * n_chips :]
    dq_own_ref, dq_send_ref = refs[:2]
    dkv = refs[2 : 2 + n_chips]
    message_out = refs[2 + n_chips : 2 + 2 * n_chips]
    proj, vl, p_ref, ds_ref, dqt, ups, low_ref = refs[2 + 2 * n_chips :]
    places = Places(lens_ref, rows)
    core, chip, chip_rows = places.core, places.chip, places.chip_rows
    head_scale = HEAD_WIDTH ** (-0.5)
    parts = head_parts(chip_rows)

    for k in range(n_chips):
        for side in (0, 1):
            for i in range(2 * rank // 8):
                proj[k, 8 * i : 8 * i + 8, side * rows : (side + 1) * rows] = kv[k][side][
                    rows:, i * rows : (i + 1) * rows
                ]
    vl[...] = jnp.zeros_like(vl)
    low_ref[...] = jnp.zeros_like(low_ref)
    ups[...] = jnp.zeros_like(ups)

    def one_group(g, _):
        at_k = pl.ds(pl.multiple_of(g * HEAD_WIDTH, 128), HEAD_WIDTH)
        at_v = pl.ds(pl.multiple_of(KV_HALF + g * HEAD_WIDTH, 128), HEAD_WIDTH)
        top = functools.reduce(jnp.maximum, [ref[g, 0:1] for ref in stats])
        weight = [jnp.exp2(ref[g, 0:1] - top) for ref in stats]
        inverse = 1.0 / sum(ref[g, 1:2] * w for ref, w in zip(stats, weight))
        delta = sum(ref[g, 2:3] * w for ref, w in zip(stats, weight)) * inverse
        at_b = pl.multiple_of(core * KV_HALF + g * HEAD_WIDTH, 128)
        for k in range(n_chips):
            factor = weight[k] * inverse
            slot = k % 2
            for part in parts:
                p = e_in[k][g, :, part].astype(F32) * factor[:, part]
                p_ref[slot, :, part] = p.astype(BF16)
                ds = p * (dp_in[k][g, :, part].astype(F32) - delta[:, part])
                ds_ref[slot, :, part] = ds.astype(BF16)
            ds = ds_ref[slot]
            dv = dot_nn(p_ref[slot], gs[g]).astype(BF16)
            dkv[k][:, at_k] = (dot_nn(ds, qs[g]) * head_scale).astype(BF16)
            dkv[k][:, at_v] = dv
            if k == 0:
                dqt[...] = dot_tn(key_rows(kv[k], rows, at_k), ds)
            else:
                dqt[...] += dot_tn(key_rows(kv[k], rows, at_k), ds)
            low = dot_nt(vb_ref[:, pl.ds(at_b, HEAD_WIDTH)], dv)
            vl[(chip - k + n_chips) % n_chips] += low
        dqt[...] *= head_scale

        at_b = pl.multiple_of(core * Q_HALF + g * GROUP * HEAD_WIDTH, 128)
        for j, part in enumerate(parts):
            up = qb_ref[:, pl.ds(pl.multiple_of(at_b + j * HEAD_WIDTH, 128), HEAD_WIDTH)]
            low_ref[...] += dot_nn(up, dqt[:, part].astype(BF16))
            dq = jnp.transpose(dqt[:, part]).astype(BF16)
            at = pl.ds(pl.multiple_of((g * GROUP + j) * HEAD_WIDTH, 128), HEAD_WIDTH)
            dq_own_ref[:, at] = dq[:rows]
            dq_send_ref[:, at] = dq[rows:]
            ups[:, at] = dot_nn(proj[0, :rank], dq)
        return 0

    lax.fori_loop(0, CORE_HEADS, one_group, 0)
    total = jnp.zeros((rank, KV_HALF), F32)
    for k in range(n_chips):
        total = total + dot_nn(proj[k, rank:], dkv[k][:, KV_HALF:])
    ups[:, Q_HALF : Q_HALF + KV_HALF] = total

    for k in range(n_chips):
        message_out[k][:, :chip_rows] = low_ref[...].astype(BF16)
        for i in range(2):
            message_out[k][:, (i + 1) * chip_rows : (i + 2) * chip_rows] = vl[chip ^ k ^ i].astype(BF16)
        at = pl.multiple_of((chip ^ k) * tail, 128)
        message_out[k][:, 3 * chip_rows :] = ups[:, pl.ds(at, tail)].astype(BF16)


def adapters(n_chips, rank, *refs):
    own, far = refs[:n_chips], refs[n_chips : 2 * n_chips]
    hidden = refs[2 * n_chips : 2 * n_chips + 2]
    out_ref = refs[-1]
    chip_rows, width = hidden[0].shape
    rows = chip_rows // 2
    query, value = jnp.zeros((rank, width), F32), jnp.zeros((rank, width), F32)
    for k in range(2):
        for first, other in ((0, rows), (rows, 0)):
            tokens = hidden[k][first : first + rows]
            low = own[k][:, first : first + rows].astype(F32) + far[k][:, other : other + rows].astype(F32)
            query += dot_nn(low.astype(BF16), tokens)
            at = (k + 1) * chip_rows
            low = sum(ref[:, at + first : at + first + rows].astype(F32) for ref in own)
            low += sum(ref[:, at + other : at + other + rows].astype(F32) for ref in far)
            value += dot_nn(low.astype(BF16), tokens)
    out_ref[:, :width] = (ADAPTER_SCALE * query).astype(BF16)
    out_ref[:, width : 2 * width] = (ADAPTER_SCALE * value).astype(BF16)
    tail = sum(ref[:, 3 * chip_rows :].astype(F32) for ref in own)
    out_ref[:, 2 * width :] = (ADAPTER_SCALE * tail).astype(BF16)


def finish_adapters(n_chips, tail, *refs):
    own, far = refs[:n_chips], refs[n_chips : 2 * n_chips]
    qa_ref, qb_ref, va_ref, vb_ref, buffer = refs[-5:]
    index = lax.axis_index("ctx")
    core, chip = index % 2, index // 2
    width = qa_ref.shape[1] // 4
    for half, pieces in ((core, own), (1 - core, far)):
        for side in (0, 1):
            total = tree_sum([ref[:, : 2 * width].astype(F32) for ref in pieces[side::2]])
            at = pl.ds(pl.multiple_of((2 * half + (chip % 2 ^ side)) * width, 128), width)
            qa_ref[:, at] = total[:, :width]
            va_ref[:, at] = total[:, width:]
        for k in range(n_chips):
            at = pl.ds(pl.multiple_of((chip ^ k) * tail, 128), tail)
            buffer[:, at] = pieces[k][:, 2 * width :].astype(F32)
        qb_ref[:, pl.ds(pl.multiple_of(half * Q_HALF, 128), Q_HALF)] = buffer[:, :Q_HALF]
        vb_ref[:, pl.ds(pl.multiple_of(half * KV_HALF, 128), KV_HALF)] = buffer[:, Q_HALF : Q_HALF + KV_HALF]


def join_rows(own_ref, far_ref, out_ref):
    core = lax.axis_index("ctx") % 2
    width = own_ref.shape[1]
    out_ref[:, pl.ds(pl.multiple_of(core * width, 128), width)] = own_ref[...]
    out_ref[:, pl.ds(pl.multiple_of((1 - core) * width, 128), width)] = far_ref[...]


def join_kv(own_ref, far_ref, dk_ref, dv_ref):
    core = lax.axis_index("ctx") % 2
    rows = far_ref.shape[0]
    for i, ref in enumerate((dk_ref, dv_ref)):
        columns = slice(i * KV_HALF, (i + 1) * KV_HALF)
        ref[:, pl.ds(pl.multiple_of(core * KV_HALF, 128), KV_HALF)] = own_ref[:rows, columns]
        ref[:, pl.ds(pl.multiple_of((1 - core) * KV_HALF, 128), KV_HALF)] = far_ref[:, columns]


def tree_sum(parts):
    while len(parts) > 1:
        parts = [a + b for a, b in zip(parts[::2], parts[1::2])]
    return parts[0]


def step(query, key, value, gradient, hidden, doc_lengths, querya, queryb, valuea, valueb):
    n_ctx, n_dp = lax.axis_size("ctx"), lax.axis_size("dp")
    n_chips = n_ctx // 2
    q, k, v, g, x = query[0], key[0], value[0], gradient[0], hidden[0]
    rows, width = x.shape[0], x.shape[1] // 2
    rank = querya.shape[0]
    chip_rows = 2 * rows
    lanes = GROUP * chip_rows
    sds = jax.ShapeDtypeStruct

    def swap(a):
        return lax.ppermute(a, "ctx", [(i, i ^ 1) for i in range(n_ctx)])

    def up(a, step):
        return lax.ppermute(a, "ctx", [(i, (i + 2 * step) % n_ctx) for i in range(n_ctx)])

    def down(a, step, first=1):
        if step > 1 or first > 1:
            return up(a, -step)
        chips = range(1, n_chips)
        return lax.ppermute(a, "ctx", [(2 * i + c, 2 * (i - 1) + c) for i in chips for c in (0, 1)])

    def across(a, bit):
        return lax.ppermute(a, "dp", [(i, i ^ bit) for i in range(n_dp)])

    def along(a, bit):
        return lax.ppermute(a, "ctx", [(i, i ^ (2 * bit)) for i in range(n_ctx)])

    block = sds((rows + 2 * rank * rows // (2 * KV_HALF), 2 * KV_HALF), BF16)
    kv_own, kv_send = call(
        split_kv,
        [block] * 2,
        (k, v, x, querya, valuea),
        scratch=[
            pltpu.VMEM(x.shape, BF16),
            pltpu.VMEM((2 * rank, x.shape[1]), BF16),
            pltpu.SemaphoreType.DMA((10,)),
        ],
        hbm=range(5),
        limit=VMEM_MOST - (3 << 17),
    )
    kv = []
    for block in (kv_own, swap(kv_send)):
        chain = [block]
        if n_chips > 1:
            last = up(block, n_chips - 1)
            for _ in range(1, n_chips - 1):
                chain.append(up(chain[-1], 1))
            chain.append(last)
        kv.append(chain)
    kv = list(zip(*kv))

    pack, hidden_far = call(
        split_rest,
        [sds((rows, 2 * Q_HALF), BF16), sds((rows, width), BF16)],
        (q, g, x),
    )
    pack, hidden_far = swap(pack), swap(hidden_far)
    hiddens = call(split_hidden, [sds((chip_rows, width // 2), BF16)] * 2, (x, hidden_far))
    hiddens = [hiddens[0], along(hiddens[1], 1)]

    tail = -(-(Q_HALF + KV_HALF) // (128 * n_chips)) * 128
    tile = (CORE_HEADS, chip_rows, lanes)
    held = F32 if 8 * n_chips * math.prod(tile) <= 32 << 20 else BF16
    chunk = [sds(tile, held)] * 2 + [sds((CORE_HEADS, 8, lanes), F32)]
    stacked = sds((CORE_HEADS, lanes, HEAD_WIDTH), BF16)
    work = 2 * 2 * math.prod(tile) * HEAD_WIDTH
    chunks = [None] * n_chips
    *chunks[0], qs, gs = call(
        functools.partial(chunk_scores, 0, rows),
        chunk + [stacked] * 2,
        (doc_lengths, *kv[0], q, g, pack),
        flops=work,
        smem=(0,),
    )
    for c in range(1, n_chips):
        chunks[c] = call(
            functools.partial(chunk_scores, c, rows), chunk, (doc_lengths, *kv[c], qs, gs), flops=work, smem=(0,)
        )
    outs = (
        [sds((rows, Q_HALF), BF16)] * 2
        + [sds((chip_rows, 2 * KV_HALF), BF16)] * n_chips
        + [sds((rank, 3 * chip_rows + tail), BF16)] * n_chips
    )
    result = call(
        functools.partial(gradients, n_chips, rank, rows, tail),
        outs,
        (doc_lengths, qs, gs, queryb, valueb, *sum(kv, ()), *(c[i] for i in range(3) for c in chunks)),
        scratch=[
            pltpu.VMEM((n_chips, 2 * rank, chip_rows), BF16),
            pltpu.VMEM((n_chips, rank, chip_rows), F32),
            pltpu.VMEM((2, chip_rows, lanes), BF16),
            pltpu.VMEM((2, chip_rows, lanes), BF16),
            pltpu.VMEM((HEAD_WIDTH, lanes), F32),
            pltpu.VMEM((rank, tail * n_chips), F32),
            pltpu.VMEM((rank, chip_rows), F32),
        ],
        flops=3 * n_chips * work // 2,
        smem=(0,),
    )
    dq_own, dq_send = result[:2]
    dkv = result[2 : 2 + n_chips]
    messages = result[2 + n_chips :]

    own = [messages[0]] + [along(messages[bit], bit) for bit in range(1, n_chips)]
    far = [swap(a) for a in own]

    if n_chips > 1:
        last = down(dkv[n_chips - 1], n_chips - 1)
        total = dkv[n_chips - 2]
        for step in range(n_chips - 2, 0, -1):
            total = down(total, 1, step).astype(F32) + dkv[step - 1].astype(F32)
            total = (total if step > 1 else total + last.astype(F32)).astype(BF16)
    else:
        total = dkv[0]
    (query_grad,) = call(join_rows, [sds((rows, 2 * Q_HALF), BF16)], (dq_own, swap(dq_send)))
    dkv_far = swap(total[rows:])
    key_grad, value_grad = call(join_kv, [sds((rows, 2 * KV_HALF), BF16)] * 2, (total, dkv_far))

    (part,) = call(
        functools.partial(adapters, n_chips, rank),
        [sds((rank, width + tail), BF16)],
        (*own, *far, *hiddens),
    )
    got = [part] + [across(part, bit) for bit in range(1, n_dp)]
    part = tree_sum([a.astype(F32) for a in got]).astype(BF16)
    own = [part] + [along(part, bit) for bit in range(1, n_chips)]
    far = [swap(a) for a in own]
    qa_grad, qb_grad, va_grad, vb_grad = call(
        functools.partial(finish_adapters, n_chips, tail),
        [
            sds((rank, 2 * width), F32),
            sds((rank, 2 * Q_HALF), F32),
            sds((rank, 2 * width), F32),
            sds((rank, 2 * KV_HALF), F32),
        ],
        (*own, *far),
        scratch=[pltpu.VMEM((rank, tail * n_chips), F32)],
    )
    return (
        query_grad[None],
        key_grad[None],
        value_grad[None],
        qa_grad,
        qb_grad,
        va_grad,
        vb_grad,
    )


def solution(mesh):
    tokens = P("dp", "ctx", None)
    return jax.shard_map(
        step,
        mesh=mesh,
        in_specs=(tokens,) * 5 + (P("dp", None),) + (P(),) * 4,
        out_specs=(tokens,) * 3 + (P(),) * 4,
        check_vma=False,
    )
```
